256 devices in a mesh: shell: 8 (over z), sector: 32 (over x, y, core).
Axes of the slice: x: 4, y: 4, z: 8, core: 2. Of those that a mesh axis runs over, the one named last changes fastest.
Arguments:
- bricks: bfloat16 [8, 256, 32, 512], P('shell', 'sector'), may hold values from -6 to 6
- conv_w: bfloat16 [32, 864], replicated, may hold values from -0.21875 to 0.21875
- conv_b: float32 [32], replicated, may hold values from -3 to 3
- head_w1: bfloat16 [32, 64], replicated, may hold values from -1 to 1
- head_b1: float32 [64], replicated, may hold values from -3 to 3
- head_w2: float32 [64, 2], replicated, may hold values from -0.75 to 0.75
- queries: int32 [8, 1024, 256], P('shell', 'sector'), may hold values from -1 to 4095, as said below
- sample_src: int32 [8, 131072], P('shell', 'sector'), may hold values from 0 to 8191, as said below
- depth_target: float32 [16384], P('sector'), may hold values from 0.1 to 0.9
- inten_target: float32 [16384], P('sector'), may hold values from 0 to 1
- drop_label: int32 [16384], P('sector'), may hold values 0 or 1
Outputs:
- loss_mean: float32 [], replicated
- grad_conv_w: float32 [32, 864], replicated
- grad_conv_b: float32 [32], replicated
- grad_head_w1: float32 [32, 64], replicated
- grad_head_b1: float32 [64], replicated
- grad_head_w2: float32 [64, 2], replicated
- grad_bricks: bfloat16 [8, 256, 32, 512], P('shell', 'sector')
- ray_depth: float32 [16384], P('sector')
The draws below stay inside these ranges and needn't reach their ends.
Inputs may be any that keep to these rules, and one draw needn't show every extreme that they name: `queries`: entry of the buffer from a device of sector v to owner w: a cell address (brick of the owner times 512 plus cell) or -1 for an empty slot. Every sample of a device holds exactly one live slot, named by sample_src as w * 256 + slot. In every shell one owner receives full buffers of 256 from every sector. `sample_src`: A slot w * 256 + slot of the sample's own device; distinct samples of a device have distinct slots.
All inputs are finite; a program needn't handle non-finite values. No bound on the sum of `drop_label` on one device may be relied on, other than what follows from the above.
Results may differ from the reference program's by a relative error of at most 0.0015.
The reference program's roundings to bfloat16 on the way count: a program that leaves them out, or rounds other values in their place, can miss the bound.
Values may be sent and summed in bfloat16 or wider, within the bound.
No kernel may reach another device: no remote copies, remote signals or barrier semaphores. Data moves between devices by JAX's collectives and lax.ppermute only.
A program may use at most 192 MiB of HBM per device.

```python
import math
import jax
import jax.numpy as jnp
from jax import lax

CH = 32
HID = 64
SAMP = 8
RAY_DEV = 512
BRICK_DEV = 8
CAP = 256
RAYS = 16384
BRICKS = 256
N_SHELL = 8
N_SECTOR = 32


def build_plan(base_key):
    per_device = RAY_DEV * SAMP
    rank_list = jnp.arange(per_device, dtype=jnp.int32)

    def one_device(shell_key, source):
        device_key = jax.random.fold_in(shell_key, source + 1000)
        busiest = jax.random.randint(shell_key, (), 0, N_SECTOR, dtype=jnp.int32)
        rank_order = jax.random.permutation(jax.random.fold_in(device_key, 1), per_device).astype(jnp.int32)
        spread = rank_list - CAP
        owner_rank = jnp.where(rank_list < CAP, busiest, (busiest + 1 + spread % (N_SECTOR - 1)) % N_SECTOR)
        drawn_pos = spread // (N_SECTOR - 1)
        other_pos = jnp.where(owner_rank == N_SECTOR - 1, CAP - 1 - drawn_pos, drawn_pos)
        position = jnp.where(rank_list < CAP, rank_list, other_pos)
        address = jax.random.randint(jax.random.fold_in(device_key, 2), (per_device,), 0, BRICK_DEV * 512, dtype=jnp.int32)
        address = address.at[0].set(BRICK_DEV * 512 - 1)
        slot_index = (owner_rank * CAP + position).astype(jnp.int32)
        sources = jnp.zeros((per_device,), jnp.int32).at[rank_order].set(slot_index)
        slot_table = jnp.full((N_SECTOR * CAP,), -1, jnp.int32).at[slot_index].set(address)
        return (slot_table.reshape(N_SECTOR, CAP), sources)

    def one_shell(shell_id):
        shell_key = jax.random.fold_in(base_key, shell_id)
        return jax.vmap(lambda source: one_device(shell_key, source))(jnp.arange(N_SECTOR, dtype=jnp.int32))
    tables, sources = jax.vmap(one_shell)(jnp.arange(N_SHELL, dtype=jnp.int32))
    return (tables.reshape(N_SHELL, N_SECTOR * N_SECTOR, CAP), sources.reshape(N_SHELL, N_SECTOR * per_device))


def draw_queries(key, part):
    return build_plan(jax.random.fold_in(key, 77))[0]


def draw_sample_src(key, part):
    return build_plan(jax.random.fold_in(key, 77))[1]


def touch_ends(entries, rng, low, high):
    index_at = [jax.random.randint(jax.random.fold_in(rng, axis), (), 0, length) for axis, length in enumerate(entries.shape)]
    main_axis = entries.shape.index(max(entries.shape))
    neighbour = index_at[:main_axis] + [(index_at[main_axis] + 1) % entries.shape[main_axis]] + index_at[main_axis + 1:]
    return entries.at[tuple(index_at)].set(low).at[tuple(neighbour)].set(high)


def block_levels(rng, dims, cuts, least, top_value):
    factor_of = 1.0
    for dim, blocks in cuts:
        draws = jax.random.uniform(jax.random.fold_in(jax.random.fold_in(rng, 6), dim), (blocks,), jnp.float32, least / len(cuts), top_value / len(cuts))
        factor_of = factor_of * jnp.repeat(jnp.exp(draws), dims[dim] // blocks).reshape((-1,) + (1,) * (len(dims) - 1 - dim))
    return factor_of


def gaussian(stream_key, shape, scale, reach, cuts=(), kind=jnp.bfloat16):
    gain = block_levels(stream_key, shape, cuts, -0.22, 0.18) if cuts else 1.0
    values = jax.random.normal(stream_key, shape, jnp.float32) * scale * gain
    return jnp.minimum(jnp.maximum(values, -reach), reach).astype(kind)


def setup_inputs(seed: int = 0) -> dict:
    streams_of = jax.random.split(jax.random.key(seed), 12)
    return {
        "bricks": gaussian(streams_of[0], (N_SHELL, BRICKS, CH, 512), 1.0, 6.0, ((0, 8), (1, 32))),
        "conv_w": gaussian(streams_of[1], (CH, 27 * CH), (27 * CH) ** -0.5, 0.21875),
        "conv_b": gaussian(streams_of[2], (CH,), 0.5, 3.0, (), jnp.float32),
        "head_w1": gaussian(streams_of[3], (CH, HID), CH ** -0.5, 1.0),
        "head_b1": gaussian(streams_of[4], (HID,), 0.5, 3.0, (), jnp.float32),
        "head_w2": gaussian(streams_of[5], (HID, 2), HID ** -0.5, 0.75, (), jnp.float32),
        "queries": draw_queries(jax.random.fold_in(streams_of[11], 71), 0),
        "sample_src": draw_sample_src(jax.random.fold_in(streams_of[11], 71), 0),
        "depth_target": jnp.clip(0.1 + 0.79999997 * jax.random.uniform(streams_of[8], (RAYS,), jnp.float32) ** block_levels(streams_of[8], (RAYS,), ((0, 32),), -0.2, 0.2), 0.1, 0.9),
        "inten_target": jnp.clip(1.0 * jax.random.uniform(streams_of[9], (RAYS,), jnp.float32) ** block_levels(streams_of[9], (RAYS,), ((0, 32),), -0.2, 0.2), 0.0, 1.0),
        "drop_label": touch_ends((jax.random.randint(streams_of[10], (RAYS,), 0, 4) < 1).astype(jnp.int32), jax.random.fold_in(streams_of[10], 1), 0, 1),
    }


HIGHEST = lax.Precision.HIGHEST
CUBE_OFFSETS = [(a, b, c) for a in range(3) for b in range(3) for c in range(3)]

def unfold_cells(block_set):
    brick_count = block_set.shape[0]
    channel_width = block_set.shape[1]
    cube = block_set.reshape(brick_count, channel_width, 8, 8, 8)
    padded = jnp.pad(cube, ((0, 0), (0, 0), (1, 1), (1, 1), (1, 1)))
    columns = [padded[:, :, a:a + 8, b:b + 8, c:c + 8].reshape(brick_count, channel_width, 512) for a, b, c in CUBE_OFFSETS]
    return jnp.stack(columns, axis=1).reshape(brick_count, 27 * channel_width, 512)

def decode_exact(block_set, weight_full, bias_conv):
    pre_act = jnp.einsum('oc,bcn->bon', weight_full, unfold_cells(block_set), precision=HIGHEST) + bias_conv[None, :, None]
    return jax.nn.gelu(pre_act)

def conv_backward(block_set, block_cot, conv_w, conv_b):
    unfolded = unfold_cells(block_set)
    pre_act = jnp.einsum('oc,bcn->bon', conv_w, unfolded, preferred_element_type=jnp.float32) + conv_b[None, :, None]
    _, gelu_pull = jax.vjp(jax.nn.gelu, pre_act)
    pre_grad = gelu_pull(block_cot)[0].astype(jnp.bfloat16)
    weight_grad = jnp.einsum('bon,bcn->oc', pre_grad, unfolded, preferred_element_type=jnp.float32)
    bias_grad = lax.optimization_barrier(jnp.sum(pre_grad.astype(jnp.float32), axis=(0, 2)))
    column_grad = jnp.einsum('oc,bon->bcn', conv_w, pre_grad, preferred_element_type=jnp.float32)
    _, fold_pull = jax.vjp(unfold_cells, jnp.zeros(block_set.shape, jnp.float32))
    block_grad = fold_pull(column_grad)[0]
    return (weight_grad, bias_grad, block_grad.astype(jnp.bfloat16))

def field_head(feature_cols, weight_one, bias_one, weight_two):
    hidden = jnp.einsum('ch,cm->hm', weight_one, feature_cols, precision=HIGHEST) + bias_one[:, None]
    outputs = jnp.einsum('hk,hm->km', weight_two, jax.nn.gelu(hidden), precision=HIGHEST)
    return (jax.nn.softplus(outputs[0]), jax.nn.sigmoid(outputs[1]))

def render_terms(density, intensity, depth_grid, step_size):
    optical = density * step_size
    before = jnp.cumsum(optical, axis=-1) - optical
    weights = jnp.exp(-before) * (1.0 - jnp.exp(-optical))
    return (lax.optimization_barrier(jnp.sum(weights * depth_grid, axis=-1)), lax.optimization_barrier(jnp.sum(weights * intensity, axis=-1)), lax.optimization_barrier(jnp.sum(optical, axis=-1)))

def reference(bricks, conv_w, conv_b, head_w1, head_b1, head_w2, queries, sample_src, depth_target, inten_target, drop_label):
    weight_full = conv_w.astype(jnp.float32)
    weight_one = head_w1.astype(jnp.float32)
    group_size = math.gcd(BRICK_DEV, 8)
    per_device = RAY_DEV * SAMP
    per_shell = per_device * N_SECTOR

    def decode_shell(shell_bricks):
        groups = shell_bricks.reshape(BRICKS // group_size, group_size, CH, 512)
        result = lax.map(lambda block_set: decode_exact(block_set.astype(jnp.float32), weight_full, conv_b).astype(jnp.bfloat16), groups)
        return result.reshape(BRICKS, CH, 512)
    decoded = lax.map(decode_shell, bricks)

    def locate_cells(shell_id):
        slot_ids = sample_src[shell_id].astype(jnp.int32)
        source_ids = (jnp.arange(per_shell, dtype=jnp.int32) // per_device).astype(jnp.int32)
        owner_ids = slot_ids // CAP
        position = slot_ids % CAP
        address = queries[shell_id][source_ids * N_SECTOR + owner_ids, position]
        return (owner_ids * BRICK_DEV + address // 512, address % 512)

    def sample_features(shell_id):
        brick_ids, cell_ids = locate_cells(shell_id)
        return decoded[shell_id][brick_ids, :, cell_ids].T.astype(jnp.float32)

    def shell_forward(shell_id):
        return field_head(sample_features(shell_id), weight_one, head_b1, head_w2)
    density, intensity = lax.map(shell_forward, jnp.arange(N_SHELL, dtype=jnp.int32))
    density = density.reshape(N_SHELL, RAYS, SAMP)
    intensity = intensity.reshape(N_SHELL, RAYS, SAMP)

    def render_loss(dens_all, inten_all):
        step_size = 2.0 / (N_SHELL * SAMP)
        depth_grid = ((jnp.arange(N_SHELL * SAMP, dtype=jnp.float32).reshape(N_SHELL, SAMP) + 0.5) / (N_SHELL * SAMP))[:, None, :]
        shell_depth, shell_inten, shell_tau = render_terms(dens_all, inten_all, depth_grid, step_size)
        prefix = jnp.cumsum(shell_tau, axis=0) - shell_tau
        entry_trans = jnp.exp(-prefix)
        ray_depth = lax.optimization_barrier(jnp.sum(entry_trans * shell_depth, axis=0))
        ray_inten = lax.optimization_barrier(jnp.sum(entry_trans * shell_inten, axis=0))
        escape = jnp.exp(-lax.optimization_barrier(jnp.sum(shell_tau, axis=0)))
        dropped = drop_label.astype(jnp.float32)
        kept_weight = 1.0 - dropped
        loss_total = jnp.sum(kept_weight * ((ray_depth - depth_target) ** 2 + (ray_inten - inten_target) ** 2) + (escape - dropped) ** 2)
        return (loss_total, ray_depth)
    loss_total, render_pull, ray_depth = jax.vjp(render_loss, density, intensity, has_aux=True)
    dens_grad, inten_grad = render_pull(jnp.ones((), jnp.float32))

    def conv_back(totals, pair_in):
        block_set, block_cot = pair_in
        weight_grad, bias_grad, block_grad = conv_backward(block_set, block_cot, conv_w, conv_b)
        return ((totals[0] + weight_grad, totals[1] + bias_grad), block_grad)

    def shell_backward(carry, shell_id):
        _, head_pull = jax.vjp(field_head, sample_features(shell_id), weight_one, head_b1, head_w2)
        feature_grad, grad_one, grad_bias_one, grad_two = head_pull((dens_grad[shell_id].reshape(-1), inten_grad[shell_id].reshape(-1)))
        brick_ids, cell_ids = locate_cells(shell_id)
        cell_grad = jnp.zeros((BRICKS, CH, 512), jnp.float32).at[brick_ids, :, cell_ids].add(feature_grad.T)
        start = (jnp.zeros_like(weight_full), jnp.zeros_like(conv_b))
        groups = bricks[shell_id].reshape(BRICKS // group_size, group_size, CH, 512)
        cotangents = cell_grad.reshape(BRICKS // group_size, group_size, CH, 512)
        (weight_grad, bias_grad), brick_grads = lax.scan(conv_back, start, (groups, cotangents))
        carry = (carry[0] + weight_grad, carry[1] + bias_grad, carry[2] + grad_one, carry[3] + grad_bias_one, carry[4] + grad_two)
        return (carry, brick_grads.reshape(BRICKS, CH, 512))
    initial = (jnp.zeros_like(weight_full), jnp.zeros_like(conv_b), jnp.zeros_like(weight_one), jnp.zeros_like(head_b1), jnp.zeros_like(head_w2))
    grads, grad_bricks = lax.scan(shell_backward, initial, jnp.arange(N_SHELL, dtype=jnp.int32))
    return (loss_total / RAYS, grads[0], grads[1], grads[2], grads[3], grads[4], grad_bricks, ray_depth)
```

```python
import functools

import jax
import jax.numpy as jnp
from jax import lax
from jax.experimental import pallas as pl
from jax.experimental.pallas import tpu as pltpu
from jax.sharding import PartitionSpec as P

SAMP = 8
CELLS = 512
LANE = 128
HI = 256
GELU_C = 0.7978845608028654
GELU_A = 0.044715

F32 = jnp.float32
BF16 = jnp.bfloat16
NT = (((1,), (1,)), ((), ()))
TN = (((0,), (0,)), ((), ()))
NN = (((1,), (0,)), ((), ()))


def dot(a, b, dims=NN):
    return lax.dot_general(a, b, dims, preferred_element_type=F32)


def iota(shape, axis):
    return lax.broadcasted_iota(jnp.int32, shape, axis)


def gelu_pair(x):
    x2 = x * x
    t = jnp.tanh(GELU_C * (x + GELU_A * (x2 * x)))
    half = 0.5 * (1.0 + t)
    slope = half + 0.5 * x * (1.0 - t * t) * (GELU_C * (1.0 + 3.0 * GELU_A * x2))
    return x * half, slope


def split3(v):
    a = v.astype(BF16).astype(F32)
    r = v - a
    b = r.astype(BF16).astype(F32)
    c = (r - b).astype(BF16).astype(F32)
    return a, b, c


def split2(v):
    a = v.astype(BF16)
    return a, (v - a.astype(F32)).astype(BF16)


def column(row):
    n = row.shape[1]
    eye = iota((n, n), 0) == iota((n, n), 1)
    return jnp.sum(jnp.where(eye, row, 0.0), axis=1, keepdims=True)


def row_of(col):
    n = col.shape[0]
    eye = iota((n, n), 0) == iota((n, n), 1)
    return jnp.sum(jnp.where(eye, col, 0.0), axis=0, keepdims=True)


def moved(x, step):
    return pltpu.roll(x, (-step) % x.shape[1], 1)


def shift_cells(x, direction, stride):
    if direction == 0:
        return x
    pos = (iota((1, CELLS), 1) // stride) & 7
    ok = (pos >= 1) if direction < 0 else (pos <= 6)
    return jnp.where(ok, moved(x, direction * stride), 0.0)


def c_columns(block):
    wide = block.astype(F32)
    return jnp.concatenate([shift_cells(wide, c - 1, 1) for c in range(3)], axis=0).astype(BF16)


def ab_columns(cot):
    parts = []
    for a in range(3):
        part = shift_cells(cot, 1 - a, 64)
        for b in range(3):
            parts.append(shift_cells(part, 1 - b, 8))
    return jnp.concatenate(parts, axis=0).astype(BF16)


def decode_kernel(bricks, wf, conv_b, w1, b1, w2, dec_out, slope_out, planes_out, factor_out, e0_s, e1_s):
    count, ch = bricks.shape[0], bricks.shape[1]
    bias = column(conv_b[...])
    bias1 = column(b1[...])
    for n in range(count):
        y = dot(wf[...], c_columns(bricks[n]))
        pre = bias
        for a in range(3):
            rows = [y[(3 * a + b) * ch : (3 * a + b + 1) * ch] for b in range(3)]
            t = rows[1] + shift_cells(rows[0], -1, 8) + shift_cells(rows[2], 1, 8)
            pre = pre + shift_cells(t, a - 1, 64)
        value, slope = gelu_pair(pre)
        dec = value.astype(BF16)
        dec_out[:, n * CELLS : (n + 1) * CELLS] = dec
        slope_out[:, n * CELLS : (n + 1) * CELLS] = slope
        h = dot(w1[...], dec, TN) + bias1
        g, _ = gelu_pair(h)
        e0 = jnp.sum(w2[:, 0:1] * g, axis=0, keepdims=True)
        e1 = jnp.sum(w2[:, 1:2] * g, axis=0, keepdims=True)
        for half in range(CELLS // HI):
            at = n * (CELLS // HI) + half
            e0_s[at : at + 1, :] = e0[:, half * HI : (half + 1) * HI]
            e1_s[at : at + 1, :] = e1[:, half * HI : (half + 1) * HI]
    e0 = e0_s[...]
    e1 = e1_s[...]
    density = jnp.maximum(e0, 0.0) + jnp.log1p(jnp.exp(-jnp.abs(e0)))
    intensity = 1.0 / (1.0 + jnp.exp(-e1))
    factor_out[0] = 1.0 / (1.0 + jnp.exp(-e0))
    factor_out[1] = intensity * (1.0 - intensity)
    planes_out[...] = jnp.concatenate(split3(density) + split3(intensity), axis=0).astype(BF16)


def one_hot(low):
    return jnp.where(iota((HI, low.shape[1]), 0) == low, 1.0, 0.0).astype(BF16)


def pick(planes, groups, address):
    found = dot(planes, one_hot(address & (HI - 1)))
    mine = iota((groups, address.shape[1]), 0) == (address >> 8)
    out = []
    for v in range(2):
        p = [found[(3 * v + k) * groups : (3 * v + k + 1) * groups] for k in range(3)]
        out.append(jnp.sum(jnp.where(mine, (p[0] + p[1]) + p[2], 0.0), axis=0, keepdims=True))
    return out


def spread(rows, groups, address):
    mine = iota((groups, address.shape[1]), 0) == (address >> 8)
    stack = jnp.concatenate([jnp.where(mine, r, 0.0) for r in rows], axis=0).astype(BF16)
    return dot(stack, one_hot(address & (HI - 1)), NT)


def join_planes(acc, groups):
    out = []
    for v in range(2):
        p = [acc[(3 * v + k) * groups : (3 * v + k + 1) * groups] for k in range(3)]
        out.append((p[0] + p[1]) + p[2])
    return out


def owner_pick_kernel(addr, planes, out):
    groups = planes.shape[0] // 6

    def body(s, carry):
        pair = pick(planes[...], groups, addr[pl.ds(s, 1), :])
        for v in range(2):
            for half in range(2):
                out[s, 2 * v + half : 2 * v + half + 1, :] = pair[v][:, half * LANE : (half + 1) * LANE]
        return carry

    lax.fori_loop(0, addr.shape[0], body, 0, unroll=4)


def excl_down(x):
    n = x.shape[0]
    at = iota(x.shape, 0)
    acc = jnp.where(at >= 1, pltpu.roll(x, 1, 0), 0.0)
    step = 1
    while step < n:
        acc = acc + jnp.where(at >= step, pltpu.roll(acc, step, 0), 0.0)
        step *= 2
    return acc


def excl_up(x):
    n = x.shape[0]
    at = iota(x.shape, 0)
    acc = jnp.where(at < n - 1, pltpu.roll(x, n - 1, 0), 0.0)
    step = 1
    while step < n:
        acc = acc + jnp.where(at < n - step, pltpu.roll(acc, n - step, 0), 0.0)
        step *= 2
    return acc


def sample_depths(shape, shell, shells):
    k = iota(shape, 0).astype(F32)
    return (shell.astype(F32) * SAMP + k + 0.5) / (shells * SAMP)


def sample_kernel(shells, shell_ref, replies, slots, density_out, intensity_out, out):
    groups = replies.shape[0]
    tables = [
        jnp.concatenate([replies[:, 2 * v, :], replies[:, 2 * v + 1, :]], axis=1) for v in range(2)
    ]
    planes = jnp.concatenate(split3(tables[0]) + split3(tables[1]), axis=0).astype(BF16)
    for k in range(SAMP):
        pair = pick(planes, groups, slots[k : k + 1, :])
        density_out[k : k + 1, :] = pair[0]
        intensity_out[k : k + 1, :] = pair[1]
    density = density_out[...]
    optical = density * (2.0 / (shells * SAMP))
    weights = jnp.exp(-excl_down(optical)) * (1.0 - jnp.exp(-optical))
    depth = jnp.sum(weights * sample_depths(density.shape, shell_ref[0], shells), axis=0, keepdims=True)
    inten = jnp.sum(weights * intensity_out[...], axis=0, keepdims=True)
    tau = jnp.sum(optical, axis=0, keepdims=True)
    packed = jnp.concatenate([depth, inten, tau, jnp.zeros_like(tau)], axis=0)
    for s in range(shells):
        out[s] = packed


def render_kernel(
    shells, shell_ref, terms, density, intensity, slots, target, inten_target, drop, buckets_out, depth_out, loss_out
):
    shell = shell_ref[0]
    delta = 2.0 / (shells * SAMP)
    d_all = terms[:, 0, :]
    i_all = terms[:, 1, :]
    t_all = terms[:, 2, :]
    entry = jnp.exp(-excl_down(t_all))
    ray_depth = jnp.sum(entry * d_all, axis=0, keepdims=True)
    ray_inten = jnp.sum(entry * i_all, axis=0, keepdims=True)
    escape = jnp.exp(-jnp.sum(t_all, axis=0, keepdims=True))
    dropped = drop[...].astype(F32)
    kept = 1.0 - dropped
    depth_err = ray_depth - target[...]
    inten_err = ray_inten - inten_target[...]
    loss = kept * (depth_err * depth_err + inten_err * inten_err) + (escape - dropped) * (escape - dropped)
    loss_out[...] = jnp.where(shell == 0, jnp.sum(loss, axis=1, keepdims=True), 0.0)
    depth_out[...] = ray_depth
    grad_depth = 2.0 * kept * depth_err
    grad_inten = 2.0 * kept * inten_err
    own = (grad_depth * d_all + grad_inten * i_all) * entry
    at = iota(own.shape, 0)
    behind = jnp.sum(jnp.where(at > shell, own, 0.0), axis=0, keepdims=True)
    entry_me = jnp.sum(jnp.where(at == shell, entry, 0.0), axis=0, keepdims=True)
    grad_tau = -2.0 * (escape - dropped) * escape - behind
    gd = grad_depth * entry_me
    gi = grad_inten * entry_me
    optical = density[...] * delta
    before = jnp.exp(-excl_down(optical))
    through = jnp.exp(-optical)
    weights = before * (1.0 - through)
    pull = gd * sample_depths(optical.shape, shell, shells) + gi * intensity[...]
    dens_grad = delta * (pull * before * through - excl_up(pull * weights) + grad_tau)
    inten_grad = gi * weights
    planes = split3(dens_grad) + split3(inten_grad)
    groups = buckets_out.shape[0]
    acc = jnp.zeros((6 * groups, HI), F32)
    for k in range(SAMP):
        acc = acc + spread([p[k : k + 1, :] for p in planes], groups, slots[k : k + 1, :])
    pair = join_planes(acc, groups)
    for v in range(2):
        for half in range(2):
            buckets_out[:, 2 * v + half, :] = pair[v][:, half * LANE : (half + 1) * LANE]


def fold_lanes(x):
    total = x[:, 0:LANE]
    for k in range(1, x.shape[1] // LANE):
        total = total + x[:, k * LANE : (k + 1) * LANE]
    return total


def owner_back_kernel(
    addr, cots, factor, dec, slope, bricks, w1, b1, w2, loss, payload_out, cot_out, plane_s
):
    count, ch = bricks.shape[0], bricks.shape[1]
    hid = w1.shape[1]
    groups = factor.shape[1]
    sectors = addr.shape[0]
    for v in range(2):
        whole = jnp.concatenate([cots[:, 2 * v, :], cots[:, 2 * v + 1, :]], axis=1)
        for k, part in enumerate(split3(whole)):
            plane_s[3 * v + k] = part

    def body(s, acc):
        rows = [plane_s[k, pl.ds(s, 1), :] for k in range(6)]
        return acc + spread(rows, groups, addr[pl.ds(s, 1), :])

    acc = lax.fori_loop(0, sectors, body, jnp.zeros((6 * groups, HI), F32), unroll=4)
    pair = join_planes(acc, groups)
    ge = [pair[v] * factor[v] for v in range(2)]
    bias1 = column(b1[...])
    w2_0, w2_1 = w2[:, 0:1], w2[:, 1:2]
    per = CELLS // HI
    acc_w1 = jnp.zeros((ch, hid), F32)
    acc_b1 = jnp.zeros((hid, LANE), F32)
    acc_w20 = jnp.zeros((hid, LANE), F32)
    acc_w21 = jnp.zeros((hid, LANE), F32)
    acc_cb = jnp.zeros((ch, LANE), F32)
    acc_cw = jnp.zeros((9 * ch, 3 * ch), F32)
    for n in range(count):
        cells = slice(n * CELLS, (n + 1) * CELLS)
        rows = [
            jnp.concatenate([ge[v][n * per + k : n * per + k + 1] for k in range(per)], axis=1)
            for v in range(2)
        ]
        dec_n = dec[:, cells]
        g, gs = gelu_pair(dot(w1[...], dec_n, TN) + bias1)
        dh = (w2_0 * rows[0] + w2_1 * rows[1]) * gs
        acc_b1 = acc_b1 + fold_lanes(dh)
        acc_w20 = acc_w20 + fold_lanes(g * rows[0])
        acc_w21 = acc_w21 + fold_lanes(g * rows[1])
        dh_a, dh_b = split2(dh)
        acc_w1 = acc_w1 + (dot(dec_n, dh_a, NT) + dot(dec_n, dh_b, NT))
        df = dot(w1[...], dh_a) + dot(w1[...], dh_b)
        cot = (df * slope[:, cells]).astype(BF16)
        cot_out[:, cells] = cot
        wide = cot.astype(F32)
        acc_cb = acc_cb + fold_lanes(wide)
        acc_cw = acc_cw + dot(ab_columns(wide), c_columns(bricks[n]), NT)
    lane = iota((ch, LANE), 1)
    tiles = [jnp.zeros((ch, LANE), F32) for _ in range(7)]
    pad = jnp.zeros((ch, LANE - 3 * ch), F32)
    for ab in range(9):
        block = jnp.concatenate([acc_cw[ab * ch : (ab + 1) * ch], pad], axis=1)
        tile, off = divmod(3 * ch * ab, LANE)
        if off == 0:
            tiles[tile] = tiles[tile] + block
        else:
            turned = pltpu.roll(block, off, 1)
            tiles[tile] = tiles[tile] + jnp.where(lane >= off, turned, 0.0)
            if tile + 1 < 7:
                tiles[tile + 1] = tiles[tile + 1] + jnp.where(lane < off, turned, 0.0)
    for k in range(7):
        payload_out[:, k, :] = tiles[k]
    small = [
        row_of(jnp.sum(acc_b1, axis=1, keepdims=True)),
        row_of(jnp.sum(acc_w20, axis=1, keepdims=True)),
        row_of(jnp.sum(acc_w21, axis=1, keepdims=True)),
        jnp.concatenate(
            [row_of(jnp.sum(acc_cb, axis=1, keepdims=True)), jnp.zeros((1, hid - ch), F32)], axis=1
        ),
        jnp.broadcast_to(loss[...], (1, hid)),
        jnp.zeros((ch - 5, hid), F32),
    ]
    payload_out[:, 7, :] = jnp.concatenate([acc_w1, jnp.concatenate(small, axis=0)], axis=1)


def bricks_back_kernel(cot, wf, out):
    count, ch = out.shape[0], out.shape[1]
    for n in range(count):
        wide = cot[:, n * CELLS : (n + 1) * CELLS].astype(F32)
        z = dot(wf[...], ab_columns(wide), TN)
        total = z[ch : 2 * ch]
        total = total + shift_cells(z[0:ch], 1, 1) + shift_cells(z[2 * ch : 3 * ch], -1, 1)
        out[n] = total.astype(BF16)


def add_kernel(values, out):
    total = values[0]
    for k in range(1, values.shape[0]):
        total = total + values[k]
    for k in range(out.shape[0]):
        out[k] = total


def finish_kernel(rays, values, cw_out, cb_out, w1_out, b1_out, w2_out, loss_out):
    ch = values.shape[0]
    hid = b1_out.shape[1]
    for k in range(7):
        width = min(LANE, cw_out.shape[1] - k * LANE)
        cw_out[:, k * LANE : k * LANE + width] = values[:, k, 0:width]
    small = values[:, 7, :]
    w1_out[...] = small[:, 0:hid]
    turned = pltpu.roll(small, LANE - hid, 1)
    b1_out[...] = turned[0:1, 0:hid]
    w2_out[...] = jnp.concatenate([column(turned[1:2, 0:hid]), column(turned[2:3, 0:hid])], axis=1)
    cb_out[...] = turned[3:4, 0:ch]
    loss_out[...] = turned[4:5, 0:1] * (1.0 / rays)


VMEM = pl.BlockSpec(memory_space=pltpu.VMEM)
SMEM = pl.BlockSpec(memory_space=pltpu.SMEM)


def call(kernel, shapes, specs, args, scratch=(), name=None, flops=0, moved_bytes=0):
    shapes = [jax.ShapeDtypeStruct(s, t) for s, t in shapes]
    return pl.pallas_call(
        kernel,
        out_shape=shapes,
        in_specs=specs,
        out_specs=[VMEM] * len(shapes),
        scratch_shapes=list(scratch),
        name=name,
        cost_estimate=pl.CostEstimate(flops=flops, bytes_accessed=moved_bytes, transcendentals=0),
        compiler_params=pltpu.CompilerParams(vmem_limit_bytes=40 * 1024 * 1024),
    )(*args)


def swap(value, axis):
    return lax.all_to_all(value, axis, split_axis=0, concat_axis=0, tiled=True)


def local(
    bricks, conv_w, conv_b, head_w1, head_b1, head_w2, queries, sample_src, depth_target, inten_target, drop_label
):
    shells = lax.axis_size("shell")
    sectors = lax.axis_size("sector")
    shell = lax.axis_index("shell").astype(jnp.int32).reshape(1)
    blocks = bricks[0]
    count, ch = blocks.shape[0], blocks.shape[1]
    hid = head_w1.shape[1]
    cells = count * CELLS
    groups = cells // HI
    rays = depth_target.shape[0]
    addr = swap(queries[0], "sector")
    wf = conv_w.reshape(ch, 9, 3 * ch).transpose(1, 0, 2).reshape(9 * ch, 3 * ch)
    b1 = head_b1.reshape(1, hid)
    slots = sample_src[0].reshape(rays, SAMP).T
    dec, slope, planes, factor = call(
        decode_kernel,
        [((ch, cells), BF16), ((ch, cells), F32), ((6 * groups, HI), BF16), ((2, groups, HI), F32)],
        [VMEM] * 6,
        (blocks, wf, conv_b.reshape(1, ch), head_w1, b1, head_w2),
        scratch=[pltpu.VMEM((groups, HI), F32), pltpu.VMEM((groups, HI), F32)],
        name="decode",
        flops=2 * 10**9,
        moved_bytes=2 * 10**6,
    )
    (picked,) = call(
        owner_pick_kernel,
        [((sectors, 4, LANE), F32)],
        [VMEM] * 2,
        (addr, planes),
        name="owner_pick",
        flops=10**9,
        moved_bytes=10**5,
    )
    replies = swap(picked, "sector")
    density, intensity, terms = call(
        functools.partial(sample_kernel, shells),
        [((SAMP, rays), F32), ((SAMP, rays), F32), ((shells, 4, rays), F32)],
        [SMEM, VMEM, VMEM],
        (shell, replies, slots),
        name="sample",
        flops=10**9,
        moved_bytes=10**5,
    )
    terms = swap(terms, "shell")
    buckets, ray_depth, loss = call(
        functools.partial(render_kernel, shells),
        [((sectors, 4, LANE), F32), ((1, rays), F32), ((1, 1), F32)],
        [SMEM] + [VMEM] * 7,
        (
            shell,
            terms,
            density,
            intensity,
            slots,
            depth_target.reshape(1, rays),
            inten_target.reshape(1, rays),
            drop_label.reshape(1, rays),
        ),
        name="render",
        flops=10**9,
        moved_bytes=10**5,
    )
    cots = swap(buckets, "sector")
    payload, conv_cot = call(
        owner_back_kernel,
        [((ch, 8, LANE), F32), ((ch, cells), BF16)],
        [VMEM] * 10,
        (addr, cots, factor, dec, slope, blocks, head_w1, b1, head_w2, loss),
        scratch=[pltpu.VMEM((6, sectors, HI), F32)],
        name="owner_back",
        flops=2 * 10**9,
        moved_bytes=2 * 10**6,
    )
    share = (ch * 8 // sectors, LANE)
    part = swap(payload.reshape((sectors,) + share), "sector")
    (brick_grads,) = call(
        bricks_back_kernel,
        [(blocks.shape, BF16)],
        [VMEM] * 2,
        (conv_cot, wf),
        name="bricks_back",
        flops=2 * 10**9,
        moved_bytes=10**6,
    )
    (part,) = call(add_kernel, [((shells,) + share, F32)], [VMEM], (part,), name="add_sectors")
    part = swap(part, "shell")
    (part,) = call(add_kernel, [((sectors,) + share, F32)], [VMEM], (part,), name="add_shells")
    whole = swap(part, "sector").reshape(ch, 8, LANE)
    conv_grad, conv_b_grad, grad_one, grad_b1, grad_two, loss_mean = call(
        functools.partial(finish_kernel, rays * sectors),
        [
            (conv_w.shape, F32),
            ((1, ch), F32),
            (head_w1.shape, F32),
            ((1, hid), F32),
            (head_w2.shape, F32),
            ((1, 1), F32),
        ],
        [VMEM],
        (whole,),
        name="finish",
    )
    return (
        loss_mean.reshape(()),
        conv_grad,
        conv_b_grad.reshape(ch),
        grad_one,
        grad_b1.reshape(hid),
        grad_two,
        brick_grads[None],
        ray_depth.reshape(rays),
    )


def solution(mesh):
    return jax.shard_map(
        local,
        mesh=mesh,
        in_specs=(
            P("shell", "sector", None, None),
            P(),
            P(),
            P(),
            P(),
            P(),
            P("shell", "sector", None),
            P("shell", "sector"),
            P("sector"),
            P("sector"),
            P("sector"),
        ),
        out_specs=(P(), P(), P(), P(), P(), P(), P("shell", "sector", None, None), P("sector")),
        check_vma=False,
    )
```

```python
import functools

import jax
import jax.numpy as jnp
from jax import lax
from jax.experimental import pallas as pl
from jax.experimental.pallas import tpu as pltpu
from jax.sharding import PartitionSpec as P

SAMP = 8
CELLS = 512
LANE = 128
HI = 256
GELU_C = 0.7978845608028654
GELU_A = 0.044715

F32 = jnp.float32
BF16 = jnp.bfloat16
NT = (((1,), (1,)), ((), ()))
TN = (((0,), (0,)), ((), ()))
NN = (((1,), (0,)), ((), ()))


def dot(a, b, dims=NN):
    return lax.dot_general(a, b, dims, preferred_element_type=F32)


def iota(shape, axis):
    return lax.broadcasted_iota(jnp.int32, shape, axis)


def gelu_pair(x):
    x2 = x * x
    t = jnp.tanh(GELU_C * (x + GELU_A * (x2 * x)))
    half = 0.5 * (1.0 + t)
    slope = half + 0.5 * x * (1.0 - t * t) * (GELU_C * (1.0 + 3.0 * GELU_A * x2))
    return x * half, slope


def split3(v):
    a = v.astype(BF16).astype(F32)
    r = v - a
    b = r.astype(BF16).astype(F32)
    c = (r - b).astype(BF16).astype(F32)
    return a, b, c


def split2(v):
    a = v.astype(BF16)
    return a, (v - a.astype(F32)).astype(BF16)


def column(row):
    n = row.shape[1]
    eye = iota((n, n), 0) == iota((n, n), 1)
    return jnp.sum(jnp.where(eye, row, 0.0), axis=1, keepdims=True)


def row_of(col):
    n = col.shape[0]
    eye = iota((n, n), 0) == iota((n, n), 1)
    return jnp.sum(jnp.where(eye, col, 0.0), axis=0, keepdims=True)


def moved(x, step):
    return pltpu.roll(x, (-step) % x.shape[1], 1)


def shift_cells(x, direction, stride):
    if direction == 0:
        return x
    pos = (iota((1, CELLS), 1) // stride) & 7
    ok = (pos >= 1) if direction < 0 else (pos <= 6)
    return jnp.where(ok, moved(x, direction * stride), 0.0)


def c_columns(block):
    wide = block.astype(F32)
    return jnp.concatenate([shift_cells(wide, c - 1, 1) for c in range(3)], axis=0).astype(BF16)


def ab_columns(cot):
    parts = []
    for a in range(3):
        part = shift_cells(cot, 1 - a, 64)
        for b in range(3):
            parts.append(shift_cells(part, 1 - b, 8))
    return jnp.concatenate(parts, axis=0).astype(BF16)


def offset_rows(conv_w):
    ch = conv_w.shape[0]
    width = 3 * ch
    wide = conv_w[...].astype(F32)
    tiles = [wide[:, k * LANE : (k + 1) * LANE] for k in range(wide.shape[1] // LANE)]
    lane = iota((ch, LANE), 1)
    rows = []
    for ab in range(9):
        tile, off = divmod(width * ab, LANE)
        if off == 0:
            rows.append(wide[:, tile * LANE : tile * LANE + width])
            continue
        block = pltpu.roll(tiles[tile], LANE - off, 1)
        if off + width > LANE:
            block = jnp.where(lane < LANE - off, block, pltpu.roll(tiles[tile + 1], LANE - off, 1))
        rows.append(block[:, 0:width])
    return jnp.concatenate(rows, axis=0).astype(BF16)


def decode_kernel(bricks, conv_w, conv_b, w1, b1, w2t, dec_out, slope_out, planes_out, factor_out, e0_s, e1_s):
    count, ch = bricks.shape[0], bricks.shape[1]
    bias = column(conv_b[...])
    bias1 = column(b1[...])
    w2_0, w2_1 = column(w2t[0:1, :]), column(w2t[1:2, :])
    wf = offset_rows(conv_w)
    for n in range(count):
        y = dot(wf, c_columns(bricks[n]))
        pre = bias
        for a in range(3):
            rows = [y[(3 * a + b) * ch : (3 * a + b + 1) * ch] for b in range(3)]
            t = rows[1] + shift_cells(rows[0], -1, 8) + shift_cells(rows[2], 1, 8)
            pre = pre + shift_cells(t, a - 1, 64)
        value, slope = gelu_pair(pre)
        dec = value.astype(BF16)
        dec_out[:, n * CELLS : (n + 1) * CELLS] = dec
        slope_out[:, n * CELLS : (n + 1) * CELLS] = slope
        g = gelu_pair(dot(w1[...], dec, TN) + bias1)[0]
        e0 = jnp.sum(w2_0 * g, axis=0, keepdims=True)
        e1 = jnp.sum(w2_1 * g, axis=0, keepdims=True)
        for half in range(CELLS // HI):
            at = n * (CELLS // HI) + half
            e0_s[at : at + 1, :] = e0[:, half * HI : (half + 1) * HI]
            e1_s[at : at + 1, :] = e1[:, half * HI : (half + 1) * HI]
    e0 = e0_s[...]
    e1 = e1_s[...]
    density = jnp.maximum(e0, 0.0) + jnp.log1p(jnp.exp(-jnp.abs(e0)))
    intensity = 1.0 / (1.0 + jnp.exp(-e1))
    factor_out[0] = 1.0 / (1.0 + jnp.exp(-e0))
    factor_out[1] = intensity * (1.0 - intensity)
    planes_out[...] = jnp.concatenate(split3(density) + split3(intensity), axis=0).astype(BF16)


def rays_last(sources):
    width = SAMP * LANE // 2
    rays = sources.shape[1] // SAMP
    lane = iota((SAMP, width), 1)
    mine = (lane & (SAMP - 1)) == iota((SAMP, width), 0)
    chosen = (iota((width, LANE // 2), 0) >> 3) == iota((width, LANE // 2), 1)
    chosen = jnp.where(chosen, 1.0, 0.0).astype(BF16)
    blocks = [jnp.where(mine, sources[:, k * width : (k + 1) * width], 0) for k in range(2 * rays // LANE)]
    stack = jnp.concatenate(blocks, axis=0)
    high = dot((stack >> 8).astype(F32).astype(BF16), chosen)
    low = dot((stack & 255).astype(F32).astype(BF16), chosen)
    whole = (high * 256.0 + low).astype(jnp.int32)
    parts = [whole[k * SAMP : (k + 1) * SAMP] for k in range(2 * rays // LANE)]
    return jnp.concatenate(parts, axis=1)


def arrange_kernel(target, inten_target, drop, sources, targets_out, slots_out):
    targets_out[0:1, :] = target[...]
    targets_out[1:2, :] = inten_target[...]
    targets_out[2:3, :] = drop[...].astype(F32)
    slots_out[...] = rays_last(sources)


def one_hot(low):
    return jnp.where(iota((HI, low.shape[1]), 0) == low, 1.0, 0.0).astype(BF16)


def pick(planes, groups, address):
    found = dot(planes, one_hot(address & (HI - 1)))
    mine = iota((groups, address.shape[1]), 0) == (address >> 8)
    out = []
    for v in range(2):
        p = [found[(3 * v + k) * groups : (3 * v + k + 1) * groups] for k in range(3)]
        out.append(jnp.sum(jnp.where(mine, (p[0] + p[1]) + p[2], 0.0), axis=0, keepdims=True))
    return out


def spread(rows, groups, address):
    mine = iota((groups, address.shape[1]), 0) == (address >> 8)
    stack = jnp.concatenate([jnp.where(mine, r, 0.0) for r in rows], axis=0).astype(BF16)
    return dot(stack, one_hot(address & (HI - 1)), NT)


def join_planes(acc, groups):
    out = []
    for v in range(2):
        p = [acc[(3 * v + k) * groups : (3 * v + k + 1) * groups] for k in range(3)]
        out.append((p[0] + p[1]) + p[2])
    return out


def owner_pick_kernel(addr, planes, out):
    groups = planes.shape[0] // 6
    for s in range(addr.shape[0]):
        pair = pick(planes[...], groups, addr[s])
        for v in range(2):
            for half in range(2):
                out[s, 2 * v + half : 2 * v + half + 1, :] = pair[v][:, half * LANE : (half + 1) * LANE]


def excl_down(x):
    n = x.shape[0]
    at = iota(x.shape, 0)
    acc = jnp.where(at >= 1, pltpu.roll(x, 1, 0), 0.0)
    step = 1
    while step < n:
        acc = acc + jnp.where(at >= step, pltpu.roll(acc, step, 0), 0.0)
        step *= 2
    return acc


def excl_up(x):
    n = x.shape[0]
    at = iota(x.shape, 0)
    acc = jnp.where(at < n - 1, pltpu.roll(x, n - 1, 0), 0.0)
    step = 1
    while step < n:
        acc = acc + jnp.where(at < n - step, pltpu.roll(acc, n - step, 0), 0.0)
        step *= 2
    return acc


def sample_depths(shape, shell, shells):
    k = iota(shape, 0).astype(F32)
    return (shell.astype(F32) * SAMP + k + 0.5) / (shells * SAMP)


def sample_kernel(shells, shell_ref, replies, slots, density_out, intensity_out, out):
    groups = replies.shape[0]
    tables = [
        jnp.concatenate([replies[:, 2 * v, :], replies[:, 2 * v + 1, :]], axis=1) for v in range(2)
    ]
    planes = jnp.concatenate(split3(tables[0]) + split3(tables[1]), axis=0).astype(BF16)
    for k in range(SAMP):
        pair = pick(planes, groups, slots[k : k + 1, :])
        density_out[k : k + 1, :] = pair[0]
        intensity_out[k : k + 1, :] = pair[1]
    density = density_out[...]
    optical = density * (2.0 / (shells * SAMP))
    weights = jnp.exp(-excl_down(optical)) * (1.0 - jnp.exp(-optical))
    depth = jnp.sum(weights * sample_depths(density.shape, shell_ref[0], shells), axis=0, keepdims=True)
    inten = jnp.sum(weights * intensity_out[...], axis=0, keepdims=True)
    tau = jnp.sum(optical, axis=0, keepdims=True)
    packed = jnp.concatenate([depth, inten, tau, jnp.zeros_like(tau)], axis=0)
    for s in range(shells):
        out[s] = packed


def render_kernel(
    shells, shell_ref, terms, density, intensity, slots, targets, buckets_out, depth_out, loss_out
):
    shell = shell_ref[0]
    delta = 2.0 / (shells * SAMP)
    d_all = terms[:, 0, :]
    i_all = terms[:, 1, :]
    t_all = terms[:, 2, :]
    entry = jnp.exp(-excl_down(t_all))
    ray_depth = jnp.sum(entry * d_all, axis=0, keepdims=True)
    ray_inten = jnp.sum(entry * i_all, axis=0, keepdims=True)
    escape = jnp.exp(-jnp.sum(t_all, axis=0, keepdims=True))
    dropped = targets[2:3, :]
    kept = 1.0 - dropped
    depth_err = ray_depth - targets[0:1, :]
    inten_err = ray_inten - targets[1:2, :]
    loss = kept * (depth_err * depth_err + inten_err * inten_err) + (escape - dropped) * (escape - dropped)
    loss_out[...] = jnp.where(shell == 0, jnp.sum(loss, axis=1, keepdims=True), 0.0)
    depth_out[...] = ray_depth
    grad_depth = 2.0 * kept * depth_err
    grad_inten = 2.0 * kept * inten_err
    own = (grad_depth * d_all + grad_inten * i_all) * entry
    at = iota(own.shape, 0)
    behind = jnp.sum(jnp.where(at > shell, own, 0.0), axis=0, keepdims=True)
    entry_me = jnp.sum(jnp.where(at == shell, entry, 0.0), axis=0, keepdims=True)
    grad_tau = -2.0 * (escape - dropped) * escape - behind
    gd = grad_depth * entry_me
    gi = grad_inten * entry_me
    optical = density[...] * delta
    before = jnp.exp(-excl_down(optical))
    through = jnp.exp(-optical)
    weights = before * (1.0 - through)
    pull = gd * sample_depths(optical.shape, shell, shells) + gi * intensity[...]
    dens_grad = delta * (pull * before * through - excl_up(pull * weights) + grad_tau)
    inten_grad = gi * weights
    planes = split3(dens_grad) + split3(inten_grad)
    groups = buckets_out.shape[0]
    acc = jnp.zeros((6 * groups, HI), F32)
    for k in range(SAMP):
        acc = acc + spread([p[k : k + 1, :] for p in planes], groups, slots[k : k + 1, :])
    pair = join_planes(acc, groups)
    for v in range(2):
        for half in range(2):
            buckets_out[:, 2 * v + half, :] = pair[v][:, half * LANE : (half + 1) * LANE]


def fold_lanes(x):
    total = x[:, 0:LANE]
    for k in range(1, x.shape[1] // LANE):
        total = total + x[:, k * LANE : (k + 1) * LANE]
    return total


def owner_back_kernel(
    addr, cots, factor, dec, slope, bricks, w1, b1, w2t, loss, payload_out, cot_out, plane_s
):
    count, ch = bricks.shape[0], bricks.shape[1]
    hid = w1.shape[1]
    groups = factor.shape[1]
    sectors = addr.shape[0]
    for v in range(2):
        whole = jnp.concatenate([cots[:, 2 * v, :], cots[:, 2 * v + 1, :]], axis=1)
        for k, part in enumerate(split3(whole)):
            plane_s[3 * v + k] = part

    def body(s, acc):
        return acc + spread([plane_s[k, pl.ds(s, 1), :] for k in range(6)], groups, addr[s])

    acc = lax.fori_loop(0, sectors, body, jnp.zeros((6 * groups, HI), F32), unroll=16)
    pair = join_planes(acc, groups)
    ge = [pair[v] * factor[v] for v in range(2)]
    bias1 = column(b1[...])
    w2_0, w2_1 = column(w2t[0:1, :]), column(w2t[1:2, :])
    per = CELLS // HI
    acc_w1 = jnp.zeros((ch, hid), F32)
    acc_b1 = jnp.zeros((hid, LANE), F32)
    acc_w20 = jnp.zeros((hid, LANE), F32)
    acc_w21 = jnp.zeros((hid, LANE), F32)
    acc_cb = jnp.zeros((ch, LANE), F32)
    acc_cw = jnp.zeros((9 * ch, 3 * ch), F32)
    for n in range(count):
        cells = slice(n * CELLS, (n + 1) * CELLS)
        rows = [
            jnp.concatenate([ge[v][n * per + k : n * per + k + 1] for k in range(per)], axis=1)
            for v in range(2)
        ]
        dec_n = dec[:, cells]
        g, gs = gelu_pair(dot(w1[...], dec_n, TN) + bias1)
        dh = (w2_0 * rows[0] + w2_1 * rows[1]) * gs
        acc_b1 = acc_b1 + fold_lanes(dh)
        acc_w20 = acc_w20 + fold_lanes(g * rows[0])
        acc_w21 = acc_w21 + fold_lanes(g * rows[1])
        dh_a, dh_b = split2(dh)
        acc_w1 = acc_w1 + (dot(dec_n, dh_a, NT) + dot(dec_n, dh_b, NT))
        df = dot(w1[...], dh_a) + dot(w1[...], dh_b)
        cot = (df * slope[:, cells]).astype(BF16)
        cot_out[:, cells] = cot
        wide = cot.astype(F32)
        acc_cb = acc_cb + fold_lanes(wide)
        acc_cw = acc_cw + dot(ab_columns(wide), c_columns(bricks[n]), NT)
    lane = iota((ch, LANE), 1)
    tiles = [jnp.zeros((ch, LANE), F32) for _ in range(7)]
    pad = jnp.zeros((ch, LANE - 3 * ch), F32)
    for ab in range(9):
        block = jnp.concatenate([acc_cw[ab * ch : (ab + 1) * ch], pad], axis=1)
        tile, off = divmod(3 * ch * ab, LANE)
        if off == 0:
            tiles[tile] = tiles[tile] + block
        else:
            turned = pltpu.roll(block, off, 1)
            tiles[tile] = tiles[tile] + jnp.where(lane >= off, turned, 0.0)
            if tile + 1 < 7:
                tiles[tile + 1] = tiles[tile + 1] + jnp.where(lane < off, turned, 0.0)
    for k in range(7):
        payload_out[:, k, :] = tiles[k]
    small = [
        row_of(jnp.sum(acc_b1, axis=1, keepdims=True)),
        row_of(jnp.sum(acc_w20, axis=1, keepdims=True)),
        row_of(jnp.sum(acc_w21, axis=1, keepdims=True)),
        jnp.concatenate(
            [row_of(jnp.sum(acc_cb, axis=1, keepdims=True)), jnp.zeros((1, hid - ch), F32)], axis=1
        ),
        jnp.broadcast_to(loss[...], (1, hid)),
        jnp.zeros((ch - 5, hid), F32),
    ]
    payload_out[:, 7, :] = jnp.concatenate([acc_w1, jnp.concatenate(small, axis=0)], axis=1)


def bricks_back_kernel(cot, conv_w, out):
    count, ch = out.shape[0], out.shape[1]
    wf = offset_rows(conv_w)
    for n in range(count):
        wide = cot[:, n * CELLS : (n + 1) * CELLS].astype(F32)
        z = dot(wf, ab_columns(wide), TN)
        total = z[ch : 2 * ch]
        total = total + shift_cells(z[0:ch], 1, 1) + shift_cells(z[2 * ch : 3 * ch], -1, 1)
        out[n] = total.astype(BF16)


def add_kernel(values, out):
    total = values[0]
    for k in range(1, values.shape[0]):
        total = total + values[k]
    for k in range(out.shape[0]):
        out[k] = total


def finish_kernel(rays, values, cw_out, cb_out, w1_out, b1_out, w2_out, loss_out):
    ch = values.shape[0]
    hid = b1_out.shape[1]
    for k in range(7):
        width = min(LANE, cw_out.shape[1] - k * LANE)
        cw_out[:, k * LANE : k * LANE + width] = values[:, k, 0:width]
    small = values[:, 7, :]
    w1_out[...] = small[:, 0:hid]
    turned = pltpu.roll(small, LANE - hid, 1)
    b1_out[...] = turned[0:1, 0:hid]
    w2_out[...] = turned[1:3, 0:hid]
    cb_out[...] = turned[3:4, 0:ch]
    loss_out[...] = turned[4:5, 0:1] * (1.0 / rays)


VMEM = pl.BlockSpec(memory_space=pltpu.VMEM)
SMEM = pl.BlockSpec(memory_space=pltpu.SMEM)


def call(kernel, shapes, specs, args, scratch=(), name=None, flops=0, moved_bytes=0, out_specs=None):
    shapes = [jax.ShapeDtypeStruct(s, t) for s, t in shapes]
    return pl.pallas_call(
        kernel,
        out_shape=shapes,
        in_specs=specs,
        out_specs=out_specs or [VMEM] * len(shapes),
        scratch_shapes=list(scratch),
        name=name,
        cost_estimate=pl.CostEstimate(flops=flops, bytes_accessed=moved_bytes, transcendentals=0),
        compiler_params=pltpu.CompilerParams(vmem_limit_bytes=16 * 1024 * 1024),
    )(*args)


def swap(value, axis):
    return lax.all_to_all(value, axis, split_axis=0, concat_axis=0, tiled=True)


def local(
    bricks, conv_w, conv_b, head_w1, head_b1, head_w2, queries, sample_src, depth_target, inten_target, drop_label
):
    shells = lax.axis_size("shell")
    sectors = lax.axis_size("sector")
    shell = lax.axis_index("shell").astype(jnp.int32).reshape(1)
    blocks = bricks[0]
    count, ch = blocks.shape[0], blocks.shape[1]
    hid = head_w1.shape[1]
    cells = count * CELLS
    groups = cells // HI
    rays = depth_target.shape[0]
    addr = swap(queries[0].reshape(sectors, 1, HI), "sector")
    b1 = head_b1.reshape(1, hid)
    w2t = head_w2.T
    dec, slope, planes, factor = call(
        decode_kernel,
        [((ch, cells), BF16), ((ch, cells), F32), ((6 * groups, HI), BF16), ((2, groups, HI), F32)],
        [VMEM] * 6,
        (blocks, conv_w, conv_b.reshape(1, ch), head_w1, b1, w2t),
        scratch=[pltpu.VMEM((groups, HI), F32), pltpu.VMEM((groups, HI), F32)],
        name="decode",
        flops=2 * 10**9,
        moved_bytes=2 * 10**6,
    )
    (picked,) = call(
        owner_pick_kernel,
        [((sectors, 4, LANE), F32)],
        [VMEM] * 2,
        (addr, planes),
        name="owner_pick",
        flops=10**9,
        moved_bytes=10**5,
    )
    targets, slots = call(
        arrange_kernel,
        [((3, rays), F32), ((SAMP, rays), jnp.int32)],
        [VMEM] * 4,
        (
            depth_target.reshape(1, rays),
            inten_target.reshape(1, rays),
            drop_label.reshape(1, rays),
            lax.optimization_barrier((sample_src, picked))[0],
        ),
        name="arrange",
        flops=10**9,
        moved_bytes=10**5,
    )
    replies = swap(picked, "sector")
    density, intensity, terms = call(
        functools.partial(sample_kernel, shells),
        [((SAMP, rays), F32), ((SAMP, rays), F32), ((shells, 4, rays), F32)],
        [SMEM, VMEM, VMEM],
        (shell, replies, slots),
        name="sample",
        flops=10**9,
        moved_bytes=10**5,
    )
    terms = swap(terms, "shell")
    buckets, ray_depth, loss = call(
        functools.partial(render_kernel, shells),
        [((sectors, 4, LANE), F32), ((1, rays), F32), ((1, 1), F32)],
        [SMEM] + [VMEM] * 5,
        (shell, terms, density, intensity, slots, targets),
        name="render",
        flops=10**9,
        moved_bytes=10**5,
    )
    cots = swap(buckets, "sector")
    payload, conv_cot = call(
        owner_back_kernel,
        [((ch, 8, LANE), F32), ((ch, cells), BF16)],
        [VMEM] * 10,
        (addr, cots, factor, dec, slope, blocks, head_w1, b1, w2t, loss),
        scratch=[pltpu.VMEM((6, sectors, HI), F32)],
        name="owner_back",
        flops=2 * 10**9,
        moved_bytes=2 * 10**6,
    )
    share = (ch * 8 // sectors, LANE)
    part = swap(payload.reshape((sectors,) + share), "sector")
    (brick_grads,) = call(
        bricks_back_kernel,
        [(blocks.shape, BF16)],
        [VMEM] * 2,
        (conv_cot, conv_w),
        name="bricks_back",
        flops=2 * 10**9,
        moved_bytes=10**6,
    )
    (part,) = call(add_kernel, [((shells,) + share, F32)], [VMEM], (part,), name="add_sectors")
    part = swap(part, "shell")
    (part,) = call(add_kernel, [((sectors,) + share, F32)], [VMEM], (part,), name="add_shells")
    whole = swap(part, "sector").reshape(ch, 8, LANE)
    conv_grad, conv_b_grad, grad_one, grad_b1, grad_two, loss_mean = call(
        functools.partial(finish_kernel, rays * sectors),
        [
            (conv_w.shape, F32),
            ((1, ch), F32),
            (head_w1.shape, F32),
            ((1, hid), F32),
            (w2t.shape, F32),
            ((1, 1), F32),
        ],
        [VMEM],
        (whole,),
        name="finish",
    )
    return (
        loss_mean.reshape(()),
        conv_grad,
        conv_b_grad.reshape(ch),
        grad_one,
        grad_b1.reshape(hid),
        grad_two.T,
        brick_grads[None],
        ray_depth.reshape(rays),
    )


def solution(mesh):
    return jax.shard_map(
        local,
        mesh=mesh,
        in_specs=(
            P("shell", "sector", None, None),
            P(),
            P(),
            P(),
            P(),
            P(),
            P("shell", "sector", None),
            P("shell", "sector"),
            P("sector"),
            P("sector"),
            P("sector"),
        ),
        out_specs=(P(), P(), P(), P(), P(), P(), P("shell", "sector", None, None), P("sector")),
        check_vma=False,
    )
```

```python
import functools

import jax
import jax.numpy as jnp
from jax import lax
from jax.experimental import pallas as pl
from jax.experimental.pallas import tpu as pltpu
from jax.sharding import PartitionSpec as P

SAMP = 8
CELLS = 512
LANE = 128
HI = 256
GELU_C = 0.7978845608028654
GELU_A = 0.044715

M_DECODE, M_BACK, M_GRAD, U_SPREAD = 8, 8, 4, 16

F32 = jnp.float32
BF16 = jnp.bfloat16
NT = (((1,), (1,)), ((), ()))
TN = (((0,), (0,)), ((), ()))
NN = (((1,), (0,)), ((), ()))


def dot(a, b, dims=NN):
    return lax.dot_general(a, b, dims, preferred_element_type=F32)


def iota(shape, axis):
    return lax.broadcasted_iota(jnp.int32, shape, axis)


def gelu_pair(x):
    x2 = x * x
    t = jnp.tanh(GELU_C * (x + GELU_A * (x2 * x)))
    half = 0.5 * (1.0 + t)
    slope = half + 0.5 * x * (1.0 - t * t) * (GELU_C * (1.0 + 3.0 * GELU_A * x2))
    return x * half, slope


def split3(v):
    a = v.astype(BF16).astype(F32)
    r = v - a
    b = r.astype(BF16).astype(F32)
    c = (r - b).astype(BF16).astype(F32)
    return a, b, c


def split2(v):
    a = v.astype(BF16)
    return a, (v - a.astype(F32)).astype(BF16)


def column(row):
    n = row.shape[1]
    eye = iota((n, n), 0) == iota((n, n), 1)
    return jnp.sum(jnp.where(eye, row, 0.0), axis=1, keepdims=True)


def row_of(col):
    n = col.shape[0]
    eye = iota((n, n), 0) == iota((n, n), 1)
    return jnp.sum(jnp.where(eye, col, 0.0), axis=0, keepdims=True)


def moved(x, step):
    return pltpu.roll(x, (-step) % x.shape[1], 1)


def shift_cells(x, direction, stride):
    if direction == 0:
        return x
    pos = (iota((1, x.shape[1]), 1) // stride) & 7
    ok = (pos >= 1) if direction < 0 else (pos <= 6)
    return jnp.where(ok, moved(x, direction * stride), 0.0)


def c_columns(block):
    wide = block.astype(F32)
    return jnp.concatenate([shift_cells(wide, c - 1, 1) for c in range(3)], axis=0).astype(BF16)


def ab_columns(cot):
    parts = []
    for a in range(3):
        part = shift_cells(cot, 1 - a, 64)
        for b in range(3):
            parts.append(shift_cells(part, 1 - b, 8))
    return jnp.concatenate(parts, axis=0).astype(BF16)


def offset_rows(conv_w):
    ch = conv_w.shape[0]
    width = 3 * ch
    wide = conv_w[...].astype(F32)
    tiles = [wide[:, k * LANE : (k + 1) * LANE] for k in range(wide.shape[1] // LANE)]
    lane = iota((ch, LANE), 1)
    rows = []
    for ab in range(9):
        tile, off = divmod(width * ab, LANE)
        if off == 0:
            rows.append(wide[:, tile * LANE : tile * LANE + width])
            continue
        block = pltpu.roll(tiles[tile], LANE - off, 1)
        if off + width > LANE:
            block = jnp.where(lane < LANE - off, block, pltpu.roll(tiles[tile + 1], LANE - off, 1))
        rows.append(block[:, 0:width])
    return jnp.concatenate(rows, axis=0).astype(BF16)


def side_by_side(bricks, first, number):
    return jnp.concatenate([bricks[first + n] for n in range(number)], axis=1)


def decode_kernel(bricks, conv_w, conv_b, w1, b1, w2t, dec_out, slope_out, planes_out, factor_out, e0_s, e1_s):
    count, ch = bricks.shape[0], bricks.shape[1]
    bias = column(conv_b[...])
    bias1 = column(b1[...])
    w2_0, w2_1 = column(w2t[0:1, :]), column(w2t[1:2, :])
    wf = offset_rows(conv_w)

    for first in range(0, count, M_DECODE):
        cells = slice(first * CELLS, (first + M_DECODE) * CELLS)
        y = dot(wf, c_columns(side_by_side(bricks, first, M_DECODE)))
        pre = bias
        for a in range(3):
            rows = [y[(3 * a + b) * ch : (3 * a + b + 1) * ch] for b in range(3)]
            t = rows[1] + shift_cells(rows[0], -1, 8) + shift_cells(rows[2], 1, 8)
            pre = pre + shift_cells(t, a - 1, 64)
        value, slope = gelu_pair(pre)
        dec = value.astype(BF16)
        dec_out[:, cells] = dec
        slope_out[:, cells] = slope
        g = gelu_pair(dot(w1[...], dec, TN) + bias1)[0]
        for w, e_s in ((w2_0, e0_s), (w2_1, e1_s)):
            e = jnp.sum(w * g, axis=0, keepdims=True)
            for k in range(M_DECODE * CELLS // HI):
                at = first * (CELLS // HI) + k
                e_s[at : at + 1, :] = e[:, k * HI : (k + 1) * HI]
    e0 = e0_s[...]
    e1 = e1_s[...]
    density = jnp.maximum(e0, 0.0) + jnp.log1p(jnp.exp(-jnp.abs(e0)))
    intensity = 1.0 / (1.0 + jnp.exp(-e1))
    factor_out[0] = 1.0 / (1.0 + jnp.exp(-e0))
    factor_out[1] = intensity * (1.0 - intensity)
    planes_out[...] = jnp.concatenate(split3(density) + split3(intensity), axis=0).astype(BF16)


def rays_last(sources):
    width = SAMP * LANE // 2
    rays = sources.shape[1] // SAMP
    lane = iota((SAMP, width), 1)
    mine = (lane & (SAMP - 1)) == iota((SAMP, width), 0)
    chosen = (iota((width, LANE // 2), 0) >> 3) == iota((width, LANE // 2), 1)
    chosen = jnp.where(chosen, 1.0, 0.0).astype(BF16)
    blocks = [jnp.where(mine, sources[:, k * width : (k + 1) * width], 0) for k in range(2 * rays // LANE)]
    stack = jnp.concatenate(blocks, axis=0)
    high = dot((stack >> 8).astype(F32).astype(BF16), chosen)
    low = dot((stack & 255).astype(F32).astype(BF16), chosen)
    whole = (high * 256.0 + low).astype(jnp.int32)
    parts = [whole[k * SAMP : (k + 1) * SAMP] for k in range(2 * rays // LANE)]
    return jnp.concatenate(parts, axis=1)


def arrange_kernel(target, inten_target, drop, sources, targets_out, slots_out):
    targets_out[0:1, :] = target[...]
    targets_out[1:2, :] = inten_target[...]
    targets_out[2:3, :] = drop[...].astype(F32)
    slots_out[...] = rays_last(sources)


def queries_kernel(queries, bricks, conv_w, conv_b, w1, b1, w2t, out):
    for s in range(out.shape[0]):
        out[s] = queries[s : s + 1, :]


def one_hot(low):
    return jnp.where(iota((HI, low.shape[1]), 0) == low, 1.0, 0.0).astype(BF16)


def pick(planes, groups, address):
    found = dot(planes, one_hot(address & (HI - 1)))
    mine = iota((groups, address.shape[1]), 0) == (address >> 8)
    out = []
    for v in range(2):
        p = [found[(3 * v + k) * groups : (3 * v + k + 1) * groups] for k in range(3)]
        out.append(jnp.sum(jnp.where(mine, (p[0] + p[1]) + p[2], 0.0), axis=0, keepdims=True))
    return out


def spread(rows, groups, address):
    mine = iota((groups, address.shape[1]), 0) == (address >> 8)
    stack = jnp.concatenate([jnp.where(mine, r, 0.0) for r in rows], axis=0).astype(BF16)
    return dot(stack, one_hot(address & (HI - 1)), NT)


def join_planes(acc, groups):
    out = []
    for v in range(2):
        p = [acc[(3 * v + k) * groups : (3 * v + k + 1) * groups] for k in range(3)]
        out.append((p[0] + p[1]) + p[2])
    return out


def owner_pick_kernel(addr, planes, out):
    groups = planes.shape[0] // 6
    for s in range(addr.shape[0]):
        pair = pick(planes[...], groups, addr[s])
        for v in range(2):
            for half in range(2):
                out[s, 2 * v + half : 2 * v + half + 1, :] = pair[v][:, half * LANE : (half + 1) * LANE]


def excl_down(x):
    n = x.shape[0]
    at = iota(x.shape, 0)
    acc = jnp.where(at >= 1, pltpu.roll(x, 1, 0), 0.0)
    step = 1
    while step < n:
        acc = acc + jnp.where(at >= step, pltpu.roll(acc, step, 0), 0.0)
        step *= 2
    return acc


def excl_up(x):
    n = x.shape[0]
    at = iota(x.shape, 0)
    acc = jnp.where(at < n - 1, pltpu.roll(x, n - 1, 0), 0.0)
    step = 1
    while step < n:
        acc = acc + jnp.where(at < n - step, pltpu.roll(acc, n - step, 0), 0.0)
        step *= 2
    return acc


def sample_depths(shape, shell, shells):
    k = iota(shape, 0).astype(F32)
    return (shell.astype(F32) * SAMP + k + 0.5) / (shells * SAMP)


def sample_kernel(shells, shell_ref, replies, slots, density_out, intensity_out, out):
    groups = replies.shape[0]
    tables = [
        jnp.concatenate([replies[:, 2 * v, :], replies[:, 2 * v + 1, :]], axis=1) for v in range(2)
    ]
    planes = jnp.concatenate(split3(tables[0]) + split3(tables[1]), axis=0).astype(BF16)
    for k in range(SAMP):
        pair = pick(planes, groups, slots[k : k + 1, :])
        density_out[k : k + 1, :] = pair[0]
        intensity_out[k : k + 1, :] = pair[1]
    density = density_out[...]
    optical = density * (2.0 / (shells * SAMP))
    weights = jnp.exp(-excl_down(optical)) * (1.0 - jnp.exp(-optical))
    depth = jnp.sum(weights * sample_depths(density.shape, shell_ref[0], shells), axis=0, keepdims=True)
    inten = jnp.sum(weights * intensity_out[...], axis=0, keepdims=True)
    tau = jnp.sum(optical, axis=0, keepdims=True)
    packed = jnp.concatenate([depth, inten, tau, jnp.zeros_like(tau)], axis=0)
    for s in range(shells):
        out[s] = packed


def render_kernel(
    shells, shell_ref, terms, density, intensity, slots, targets, buckets_out, depth_out, loss_out
):
    shell = shell_ref[0]
    delta = 2.0 / (shells * SAMP)
    d_all = terms[:, 0, :]
    i_all = terms[:, 1, :]
    t_all = terms[:, 2, :]
    entry = jnp.exp(-excl_down(t_all))
    ray_depth = jnp.sum(entry * d_all, axis=0, keepdims=True)
    ray_inten = jnp.sum(entry * i_all, axis=0, keepdims=True)
    escape = jnp.exp(-jnp.sum(t_all, axis=0, keepdims=True))
    dropped = targets[2:3, :]
    kept = 1.0 - dropped
    depth_err = ray_depth - targets[0:1, :]
    inten_err = ray_inten - targets[1:2, :]
    loss = kept * (depth_err * depth_err + inten_err * inten_err) + (escape - dropped) * (escape - dropped)
    loss_out[...] = jnp.where(shell == 0, jnp.sum(loss, axis=1, keepdims=True), 0.0)
    depth_out[...] = ray_depth
    grad_depth = 2.0 * kept * depth_err
    grad_inten = 2.0 * kept * inten_err
    own = (grad_depth * d_all + grad_inten * i_all) * entry
    at = iota(own.shape, 0)
    behind = jnp.sum(jnp.where(at > shell, own, 0.0), axis=0, keepdims=True)
    entry_me = jnp.sum(jnp.where(at == shell, entry, 0.0), axis=0, keepdims=True)
    grad_tau = -2.0 * (escape - dropped) * escape - behind
    gd = grad_depth * entry_me
    gi = grad_inten * entry_me
    optical = density[...] * delta
    before = jnp.exp(-excl_down(optical))
    through = jnp.exp(-optical)
    weights = before * (1.0 - through)
    pull = gd * sample_depths(optical.shape, shell, shells) + gi * intensity[...]
    dens_grad = delta * (pull * before * through - excl_up(pull * weights) + grad_tau)
    inten_grad = gi * weights
    planes = split3(dens_grad) + split3(inten_grad)
    groups = buckets_out.shape[0]
    acc = jnp.zeros((6 * groups, HI), F32)
    for k in range(SAMP):
        acc = acc + spread([p[k : k + 1, :] for p in planes], groups, slots[k : k + 1, :])
    pair = join_planes(acc, groups)
    for v in range(2):
        for half in range(2):
            buckets_out[:, 2 * v + half, :] = pair[v][:, half * LANE : (half + 1) * LANE]


def fold_lanes(x):
    total = x[:, 0:LANE]
    for k in range(1, x.shape[1] // LANE):
        total = total + x[:, k * LANE : (k + 1) * LANE]
    return total


def owner_back_kernel(
    addr, cots, factor, dec, slope, bricks, w1, b1, w2t, loss, payload_out, cot_out, plane_s, ge_s
):
    count, ch = bricks.shape[0], bricks.shape[1]
    hid = w1.shape[1]
    groups = factor.shape[1]
    sectors = addr.shape[0]
    for v in range(2):
        whole = jnp.concatenate([cots[:, 2 * v, :], cots[:, 2 * v + 1, :]], axis=1)
        for k, part in enumerate(split3(whole)):
            plane_s[3 * v + k] = part

    def body(s, acc):
        return acc + spread([plane_s[k, pl.ds(s, 1), :] for k in range(6)], groups, addr[s])

    acc = lax.fori_loop(0, sectors, body, jnp.zeros((6 * groups, HI), F32), unroll=U_SPREAD)
    pair = join_planes(acc, groups)
    for v in range(2):
        ge_s[v] = pair[v] * factor[v]
    bias1 = column(b1[...])
    w2_0, w2_1 = column(w2t[0:1, :]), column(w2t[1:2, :])
    per = CELLS // HI

    acc_w1 = jnp.zeros((ch, hid), F32)
    acc_b1 = jnp.zeros((hid, LANE), F32)
    acc_w20 = jnp.zeros((hid, LANE), F32)
    acc_w21 = jnp.zeros((hid, LANE), F32)
    acc_cb = jnp.zeros((ch, LANE), F32)
    acc_cw = jnp.zeros((9 * ch, 3 * ch), F32)
    for first in range(0, count, M_BACK):
        cells = slice(first * CELLS, (first + M_BACK) * CELLS)
        rows = [
            jnp.concatenate([ge_s[v, first * per + k : first * per + k + 1, :] for k in range(M_BACK * per)], axis=1)
            for v in range(2)
        ]
        dec_n = dec[:, cells]
        g, gs = gelu_pair(dot(w1[...], dec_n, TN) + bias1)
        dh = (w2_0 * rows[0] + w2_1 * rows[1]) * gs
        acc_b1 = acc_b1 + fold_lanes(dh)
        acc_w20 = acc_w20 + fold_lanes(g * rows[0])
        acc_w21 = acc_w21 + fold_lanes(g * rows[1])
        dh_a, dh_b = split2(dh)
        acc_w1 = acc_w1 + (dot(dec_n, dh_a, NT) + dot(dec_n, dh_b, NT))
        df = dot(w1[...], dh_a) + dot(w1[...], dh_b)
        cot = (df * slope[:, cells]).astype(BF16)
        cot_out[:, cells] = cot
        wide = cot.astype(F32)
        acc_cb = acc_cb + fold_lanes(wide)
        acc_cw = acc_cw + dot(ab_columns(wide), c_columns(side_by_side(bricks, first, M_BACK)), NT)
    lane = iota((ch, LANE), 1)
    tiles = [jnp.zeros((ch, LANE), F32) for _ in range(7)]
    pad = jnp.zeros((ch, LANE - 3 * ch), F32)
    for ab in range(9):
        block = jnp.concatenate([acc_cw[ab * ch : (ab + 1) * ch], pad], axis=1)
        tile, off = divmod(3 * ch * ab, LANE)
        if off == 0:
            tiles[tile] = tiles[tile] + block
        else:
            turned = pltpu.roll(block, off, 1)
            tiles[tile] = tiles[tile] + jnp.where(lane >= off, turned, 0.0)
            if tile + 1 < 7:
                tiles[tile + 1] = tiles[tile + 1] + jnp.where(lane < off, turned, 0.0)
    for k in range(7):
        payload_out[:, k, :] = tiles[k]
    small = [
        row_of(jnp.sum(acc_b1, axis=1, keepdims=True)),
        row_of(jnp.sum(acc_w20, axis=1, keepdims=True)),
        row_of(jnp.sum(acc_w21, axis=1, keepdims=True)),
        jnp.concatenate(
            [row_of(jnp.sum(acc_cb, axis=1, keepdims=True)), jnp.zeros((1, hid - ch), F32)], axis=1
        ),
        jnp.broadcast_to(loss[...], (1, hid)),
        jnp.zeros((ch - 5, hid), F32),
    ]
    payload_out[:, 7, :] = jnp.concatenate([acc_w1, jnp.concatenate(small, axis=0)], axis=1)


def bricks_back_kernel(cot, conv_w, out):
    count, ch = out.shape[0], out.shape[1]
    wf = offset_rows(conv_w)
    for first in range(0, count, M_GRAD):
        wide = cot[:, first * CELLS : (first + M_GRAD) * CELLS].astype(F32)
        z = dot(wf, ab_columns(wide), TN)
        total = z[ch : 2 * ch]
        total = total + shift_cells(z[0:ch], 1, 1) + shift_cells(z[2 * ch : 3 * ch], -1, 1)
        for n in range(M_GRAD):
            out[first + n] = total[:, n * CELLS : (n + 1) * CELLS].astype(BF16)


def add_kernel(values, out):
    total = values[0]
    for k in range(1, values.shape[0]):
        total = total + values[k]
    for k in range(out.shape[0]):
        out[k] = total


def finish_kernel(rays, values, cw_out, cb_out, w1_out, b1_out, w2_out, loss_out):
    ch = values.shape[0]
    hid = b1_out.shape[1]
    for k in range(7):
        width = min(LANE, cw_out.shape[1] - k * LANE)
        cw_out[:, k * LANE : k * LANE + width] = values[:, k, 0:width]
    small = values[:, 7, :]
    w1_out[...] = small[:, 0:hid]
    turned = pltpu.roll(small, LANE - hid, 1)
    b1_out[...] = turned[0:1, 0:hid]
    w2_out[...] = turned[1:3, 0:hid]
    cb_out[...] = turned[3:4, 0:ch]
    loss_out[...] = turned[4:5, 0:1] * (1.0 / rays)


VMEM = pl.BlockSpec(memory_space=pltpu.VMEM)
SMEM = pl.BlockSpec(memory_space=pltpu.SMEM)


def call(kernel, shapes, specs, args, scratch=(), name=None, flops=0, moved_bytes=0, out_specs=None):
    shapes = [jax.ShapeDtypeStruct(s, t) for s, t in shapes]
    return pl.pallas_call(
        kernel,
        out_shape=shapes,
        in_specs=specs,
        out_specs=out_specs or [VMEM] * len(shapes),
        scratch_shapes=list(scratch),
        name=name,
        cost_estimate=pl.CostEstimate(flops=flops, bytes_accessed=moved_bytes, transcendentals=0),
        compiler_params=pltpu.CompilerParams(vmem_limit_bytes=16 * 1024 * 1024),
    )(*args)


def swap(value, axis):
    return lax.all_to_all(value, axis, split_axis=0, concat_axis=0, tiled=True)


def local(
    bricks, conv_w, conv_b, head_w1, head_b1, head_w2, queries, sample_src, depth_target, inten_target, drop_label
):
    shells = lax.axis_size("shell")
    sectors = lax.axis_size("sector")
    shell = lax.axis_index("shell").astype(jnp.int32).reshape(1)
    blocks = bricks[0]
    count, ch = blocks.shape[0], blocks.shape[1]
    hid = head_w1.shape[1]
    cells = count * CELLS
    groups = cells // HI
    rays = depth_target.shape[0]
    b1 = head_b1.reshape(1, hid)
    w2t = head_w2.T
    operands = (blocks, conv_w, conv_b.reshape(1, ch), head_w1, b1, w2t)
    (asked,) = call(
        queries_kernel,
        [((sectors, 1, HI), jnp.int32)],
        [VMEM] * 7,
        (queries[0],) + operands,
        name="queries",
        moved_bytes=10**6,
    )
    addr = swap(asked, "sector")
    dec, slope, planes, factor = call(
        decode_kernel,
        [((ch, cells), BF16), ((ch, cells), F32), ((6 * groups, HI), BF16), ((2, groups, HI), F32)],
        [VMEM] * 6,
        operands,
        scratch=[pltpu.VMEM((groups, HI), F32), pltpu.VMEM((groups, HI), F32)],
        name="decode",
        flops=2 * 10**9,
        moved_bytes=2 * 10**6,
    )
    (picked,) = call(
        owner_pick_kernel,
        [((sectors, 4, LANE), F32)],
        [VMEM] * 2,
        (addr, planes),
        name="owner_pick",
        flops=10**9,
        moved_bytes=10**5,
    )
    targets, slots = call(
        arrange_kernel,
        [((3, rays), F32), ((SAMP, rays), jnp.int32)],
        [VMEM] * 4,
        (
            depth_target.reshape(1, rays),
            inten_target.reshape(1, rays),
            drop_label.reshape(1, rays),
            lax.optimization_barrier((sample_src, picked))[0],
        ),
        name="arrange",
        flops=10**9,
        moved_bytes=10**5,
    )
    replies = swap(picked, "sector")
    density, intensity, terms = call(
        functools.partial(sample_kernel, shells),
        [((SAMP, rays), F32), ((SAMP, rays), F32), ((shells, 4, rays), F32)],
        [SMEM, VMEM, VMEM],
        (shell, replies, slots),
        name="sample",
        flops=10**9,
        moved_bytes=10**5,
    )
    terms = swap(terms, "shell")
    buckets, ray_depth, loss = call(
        functools.partial(render_kernel, shells),
        [((sectors, 4, LANE), F32), ((1, rays), F32), ((1, 1), F32)],
        [SMEM] + [VMEM] * 5,
        (shell, terms, density, intensity, slots, targets),
        name="render",
        flops=10**9,
        moved_bytes=10**5,
    )
    cots = swap(buckets, "sector")
    payload, conv_cot = call(
        owner_back_kernel,
        [((ch, 8, LANE), F32), ((ch, cells), BF16)],
        [VMEM] * 10,
        (addr, cots, factor, dec, slope, blocks, head_w1, b1, w2t, loss),
        scratch=[pltpu.VMEM((6, sectors, HI), F32), pltpu.VMEM((2, groups, HI), F32)],
        name="owner_back",
        flops=2 * 10**9,
        moved_bytes=2 * 10**6,
    )
    share = (ch * 8 // sectors, LANE)
    part = swap(payload.reshape((sectors,) + share), "sector")
    (brick_grads,) = call(
        bricks_back_kernel,
        [(blocks.shape, BF16)],
        [VMEM] * 2,
        (conv_cot, conv_w),
        name="bricks_back",
        flops=2 * 10**9,
        moved_bytes=10**6,
    )
    (part,) = call(add_kernel, [((shells,) + share, F32)], [VMEM], (part,), name="add_sectors")
    part = swap(part, "shell")
    (part,) = call(add_kernel, [((sectors,) + share, F32)], [VMEM], (part,), name="add_shells")
    whole = swap(part, "sector").reshape(ch, 8, LANE)
    conv_grad, conv_b_grad, grad_one, grad_b1, grad_two, loss_mean = call(
        functools.partial(finish_kernel, rays * sectors),
        [
            (conv_w.shape, F32),
            ((1, ch), F32),
            (head_w1.shape, F32),
            ((1, hid), F32),
            (w2t.shape, F32),
            ((1, 1), F32),
        ],
        [VMEM],
        (whole,),
        name="finish",
    )
    return (
        loss_mean.reshape(()),
        conv_grad,
        conv_b_grad.reshape(ch),
        grad_one,
        grad_b1.reshape(hid),
        grad_two.T,
        brick_grads[None],
        ray_depth.reshape(rays),
    )


def solution(mesh):
    return jax.shard_map(
        local,
        mesh=mesh,
        in_specs=(
            P("shell", "sector", None, None),
            P(),
            P(),
            P(),
            P(),
            P(),
            P("shell", "sector", None),
            P("shell", "sector"),
            P("sector"),
            P("sector"),
            P("sector"),
        ),
        out_specs=(P(), P(), P(), P(), P(), P(), P("shell", "sector", None, None), P("sector")),
        check_vma=False,
    )
```

```python
import functools

import jax
import jax.numpy as jnp
from jax import lax
from jax.experimental import pallas as pl
from jax.experimental.pallas import tpu as pltpu
from jax.sharding import PartitionSpec as P

SAMP = 8
CELLS = 512
LANE = 128
HI = 256
GELU_C = 0.7978845608028654
GELU_A = 0.044715

M_DECODE, M_BACK, M_GRAD, U_SPREAD = 8, 8, 4, 16

F32 = jnp.float32
BF16 = jnp.bfloat16
NT = (((1,), (1,)), ((), ()))
TN = (((0,), (0,)), ((), ()))
NN = (((1,), (0,)), ((), ()))


def dot(a, b, dims=NN):
    return lax.dot_general(a, b, dims, preferred_element_type=F32)


def iota(shape, axis):
    return lax.broadcasted_iota(jnp.int32, shape, axis)


def gelu_pair(x):
    x2 = x * x
    t = jnp.tanh(GELU_C * (x + GELU_A * (x2 * x)))
    half = 0.5 * (1.0 + t)
    slope = half + 0.5 * x * (1.0 - t * t) * (GELU_C * (1.0 + 3.0 * GELU_A * x2))
    return x * half, slope


def split3(v):
    a = v.astype(BF16).astype(F32)
    r = v - a
    b = r.astype(BF16).astype(F32)
    c = (r - b).astype(BF16).astype(F32)
    return a, b, c


def split2(v):
    a = v.astype(BF16)
    return a, (v - a.astype(F32)).astype(BF16)


def column(row):
    n = row.shape[1]
    eye = iota((n, n), 0) == iota((n, n), 1)
    return jnp.sum(jnp.where(eye, row, 0.0), axis=1, keepdims=True)


def row_of(col):
    n = col.shape[0]
    eye = iota((n, n), 0) == iota((n, n), 1)
    return jnp.sum(jnp.where(eye, col, 0.0), axis=0, keepdims=True)


def moved(x, step):
    return pltpu.roll(x, (-step) % x.shape[1], 1)


def shift_cells(x, direction, stride):
    if direction == 0:
        return x
    pos = (iota((1, x.shape[1]), 1) // stride) & 7
    ok = (pos >= 1) if direction < 0 else (pos <= 6)
    return jnp.where(ok, moved(x, direction * stride), 0.0)


def c_columns(block):
    wide = block.astype(F32)
    return jnp.concatenate([shift_cells(wide, c - 1, 1) for c in range(3)], axis=0).astype(BF16)


def ab_columns(cot):
    parts = []
    for a in range(3):
        part = shift_cells(cot, 1 - a, 64)
        for b in range(3):
            parts.append(shift_cells(part, 1 - b, 8))
    return jnp.concatenate(parts, axis=0).astype(BF16)


def offset_rows(conv_w):
    ch = conv_w.shape[0]
    width = 3 * ch
    wide = conv_w[...].astype(F32)
    tiles = [wide[:, k * LANE : (k + 1) * LANE] for k in range(wide.shape[1] // LANE)]
    lane = iota((ch, LANE), 1)
    rows = []
    for ab in range(9):
        tile, off = divmod(width * ab, LANE)
        if off == 0:
            rows.append(wide[:, tile * LANE : tile * LANE + width])
            continue
        block = pltpu.roll(tiles[tile], LANE - off, 1)
        if off + width > LANE:
            block = jnp.where(lane < LANE - off, block, pltpu.roll(tiles[tile + 1], LANE - off, 1))
        rows.append(block[:, 0:width])
    return jnp.concatenate(rows, axis=0).astype(BF16)


def side_by_side(bricks, first, number):
    return jnp.concatenate([bricks[first + n] for n in range(number)], axis=1)


def decode_kernel(bricks, conv_w, conv_b, w1, b1, w2t, dec_out, slope_out, planes_out, factor_out, e0_s, e1_s):
    count, ch = bricks.shape[0], bricks.shape[1]
    bias = column(conv_b[...])
    bias1 = column(b1[...])
    w2_0, w2_1 = column(w2t[0:1, :]), column(w2t[1:2, :])
    wf = offset_rows(conv_w)

    for first in range(0, count, M_DECODE):
        cells = slice(first * CELLS, (first + M_DECODE) * CELLS)
        y = dot(wf, c_columns(side_by_side(bricks, first, M_DECODE)))
        pre = bias
        for a in range(3):
            rows = [y[(3 * a + b) * ch : (3 * a + b + 1) * ch] for b in range(3)]
            t = rows[1] + shift_cells(rows[0], -1, 8) + shift_cells(rows[2], 1, 8)
            pre = pre + shift_cells(t, a - 1, 64)
        value, slope = gelu_pair(pre)
        dec = value.astype(BF16)
        dec_out[:, cells] = dec
        slope_out[:, cells] = slope
        g = gelu_pair(dot(w1[...], dec, TN) + bias1)[0]
        for w, e_s in ((w2_0, e0_s), (w2_1, e1_s)):
            e = jnp.sum(w * g, axis=0, keepdims=True)
            for k in range(M_DECODE * CELLS // HI):
                at = first * (CELLS // HI) + k
                e_s[at : at + 1, :] = e[:, k * HI : (k + 1) * HI]
    e0 = e0_s[...]
    e1 = e1_s[...]
    density = jnp.maximum(e0, 0.0) + jnp.log1p(jnp.exp(-jnp.abs(e0)))
    intensity = 1.0 / (1.0 + jnp.exp(-e1))
    factor_out[0] = 1.0 / (1.0 + jnp.exp(-e0))
    factor_out[1] = intensity * (1.0 - intensity)
    planes_out[...] = jnp.concatenate(split3(density) + split3(intensity), axis=0).astype(BF16)


def rays_last(sources):
    width = SAMP * LANE // 2
    rays = sources.shape[1] // SAMP
    lane = iota((SAMP, width), 1)
    mine = (lane & (SAMP - 1)) == iota((SAMP, width), 0)
    chosen = (iota((width, LANE // 2), 0) >> 3) == iota((width, LANE // 2), 1)
    chosen = jnp.where(chosen, 1.0, 0.0).astype(BF16)
    blocks = [jnp.where(mine, sources[:, k * width : (k + 1) * width], 0) for k in range(2 * rays // LANE)]
    stack = jnp.concatenate(blocks, axis=0)
    high = dot((stack >> 8).astype(F32).astype(BF16), chosen)
    low = dot((stack & 255).astype(F32).astype(BF16), chosen)
    whole = (high * 256.0 + low).astype(jnp.int32)
    parts = [whole[k * SAMP : (k + 1) * SAMP] for k in range(2 * rays // LANE)]
    return jnp.concatenate(parts, axis=1)


def arrange_kernel(target, inten_target, drop, sources, targets_out, slots_out):
    targets_out[0:1, :] = target[...]
    targets_out[1:2, :] = inten_target[...]
    targets_out[2:3, :] = drop[...].astype(F32)
    slots_out[...] = rays_last(sources)


def one_hot(low):
    return jnp.where(iota((HI, low.shape[1]), 0) == low, 1.0, 0.0).astype(BF16)


def pick(planes, groups, address):
    found = dot(planes, one_hot(address & (HI - 1)))
    mine = iota((groups, address.shape[1]), 0) == (address >> 8)
    out = []
    for v in range(2):
        p = [found[(3 * v + k) * groups : (3 * v + k + 1) * groups] for k in range(3)]
        out.append(jnp.sum(jnp.where(mine, (p[0] + p[1]) + p[2], 0.0), axis=0, keepdims=True))
    return out


def spread(rows, groups, address):
    mine = iota((groups, address.shape[1]), 0) == (address >> 8)
    stack = jnp.concatenate([jnp.where(mine, r, 0.0) for r in rows], axis=0).astype(BF16)
    return dot(stack, one_hot(address & (HI - 1)), NT)


def join_planes(acc, groups):
    out = []
    for v in range(2):
        p = [acc[(3 * v + k) * groups : (3 * v + k + 1) * groups] for k in range(3)]
        out.append((p[0] + p[1]) + p[2])
    return out


def owner_pick_kernel(addr, planes, out):
    groups = planes.shape[0] // 6
    for s in range(addr.shape[0]):
        pair = pick(planes[...], groups, addr[s])
        for v in range(2):
            for half in range(2):
                out[s, 2 * v + half : 2 * v + half + 1, :] = pair[v][:, half * LANE : (half + 1) * LANE]


def excl_down(x):
    n = x.shape[0]
    at = iota(x.shape, 0)
    acc = jnp.where(at >= 1, pltpu.roll(x, 1, 0), 0.0)
    step = 1
    while step < n:
        acc = acc + jnp.where(at >= step, pltpu.roll(acc, step, 0), 0.0)
        step *= 2
    return acc


def excl_up(x):
    n = x.shape[0]
    at = iota(x.shape, 0)
    acc = jnp.where(at < n - 1, pltpu.roll(x, n - 1, 0), 0.0)
    step = 1
    while step < n:
        acc = acc + jnp.where(at < n - step, pltpu.roll(acc, n - step, 0), 0.0)
        step *= 2
    return acc


def sample_depths(shape, shell, shells):
    k = iota(shape, 0).astype(F32)
    return (shell.astype(F32) * SAMP + k + 0.5) / (shells * SAMP)


def sample_kernel(shells, shell_ref, replies, slots, density_out, intensity_out, out):
    groups = replies.shape[0]
    tables = [
        jnp.concatenate([replies[:, 2 * v, :], replies[:, 2 * v + 1, :]], axis=1) for v in range(2)
    ]
    planes = jnp.concatenate(split3(tables[0]) + split3(tables[1]), axis=0).astype(BF16)
    for k in range(SAMP):
        pair = pick(planes, groups, slots[k : k + 1, :])
        density_out[k : k + 1, :] = pair[0]
        intensity_out[k : k + 1, :] = pair[1]
    density = density_out[...]
    optical = density * (2.0 / (shells * SAMP))
    weights = jnp.exp(-excl_down(optical)) * (1.0 - jnp.exp(-optical))
    depth = jnp.sum(weights * sample_depths(density.shape, shell_ref[0], shells), axis=0, keepdims=True)
    inten = jnp.sum(weights * intensity_out[...], axis=0, keepdims=True)
    tau = jnp.sum(optical, axis=0, keepdims=True)
    packed = jnp.concatenate([depth, inten, tau, jnp.zeros_like(tau)], axis=0)
    for s in range(shells):
        out[s] = packed


def render_kernel(
    shells, shell_ref, terms, density, intensity, slots, targets, buckets_out, depth_out, loss_out
):
    shell = shell_ref[0]
    delta = 2.0 / (shells * SAMP)
    d_all = terms[:, 0, :]
    i_all = terms[:, 1, :]
    t_all = terms[:, 2, :]
    entry = jnp.exp(-excl_down(t_all))
    ray_depth = jnp.sum(entry * d_all, axis=0, keepdims=True)
    ray_inten = jnp.sum(entry * i_all, axis=0, keepdims=True)
    escape = jnp.exp(-jnp.sum(t_all, axis=0, keepdims=True))
    dropped = targets[2:3, :]
    kept = 1.0 - dropped
    depth_err = ray_depth - targets[0:1, :]
    inten_err = ray_inten - targets[1:2, :]
    loss = kept * (depth_err * depth_err + inten_err * inten_err) + (escape - dropped) * (escape - dropped)
    loss_out[...] = jnp.where(shell == 0, jnp.sum(loss, axis=1, keepdims=True), 0.0)
    depth_out[...] = ray_depth
    grad_depth = 2.0 * kept * depth_err
    grad_inten = 2.0 * kept * inten_err
    own = (grad_depth * d_all + grad_inten * i_all) * entry
    at = iota(own.shape, 0)
    behind = jnp.sum(jnp.where(at > shell, own, 0.0), axis=0, keepdims=True)
    entry_me = jnp.sum(jnp.where(at == shell, entry, 0.0), axis=0, keepdims=True)
    grad_tau = -2.0 * (escape - dropped) * escape - behind
    gd = grad_depth * entry_me
    gi = grad_inten * entry_me
    optical = density[...] * delta
    before = jnp.exp(-excl_down(optical))
    through = jnp.exp(-optical)
    weights = before * (1.0 - through)
    pull = gd * sample_depths(optical.shape, shell, shells) + gi * intensity[...]
    dens_grad = delta * (pull * before * through - excl_up(pull * weights) + grad_tau)
    inten_grad = gi * weights
    planes = split3(dens_grad) + split3(inten_grad)
    groups = buckets_out.shape[0]
    acc = jnp.zeros((6 * groups, HI), F32)
    for k in range(SAMP):
        acc = acc + spread([p[k : k + 1, :] for p in planes], groups, slots[k : k + 1, :])
    pair = join_planes(acc, groups)
    for v in range(2):
        for half in range(2):
            buckets_out[:, 2 * v + half, :] = pair[v][:, half * LANE : (half + 1) * LANE]


def fold_lanes(x):
    total = x[:, 0:LANE]
    for k in range(1, x.shape[1] // LANE):
        total = total + x[:, k * LANE : (k + 1) * LANE]
    return total


def owner_back_kernel(
    addr, cots, factor, dec, slope, bricks, w1, b1, w2t, loss, payload_out, cot_out, plane_s, ge_s
):
    count, ch = bricks.shape[0], bricks.shape[1]
    hid = w1.shape[1]
    groups = factor.shape[1]
    sectors = addr.shape[0]
    for v in range(2):
        whole = jnp.concatenate([cots[:, 2 * v, :], cots[:, 2 * v + 1, :]], axis=1)
        for k, part in enumerate(split3(whole)):
            plane_s[3 * v + k] = part

    def body(s, acc):
        return acc + spread([plane_s[k, pl.ds(s, 1), :] for k in range(6)], groups, addr[s])

    acc = lax.fori_loop(0, sectors, body, jnp.zeros((6 * groups, HI), F32), unroll=U_SPREAD)
    pair = join_planes(acc, groups)
    for v in range(2):
        ge_s[v] = pair[v] * factor[v]
    bias1 = column(b1[...])
    w2_0, w2_1 = column(w2t[0:1, :]), column(w2t[1:2, :])
    per = CELLS // HI

    acc_w1 = jnp.zeros((ch, hid), F32)
    acc_b1 = jnp.zeros((hid, LANE), F32)
    acc_w20 = jnp.zeros((hid, LANE), F32)
    acc_w21 = jnp.zeros((hid, LANE), F32)
    acc_cb = jnp.zeros((ch, LANE), F32)
    acc_cw = jnp.zeros((9 * ch, 3 * ch), F32)
    for first in range(0, count, M_BACK):
        cells = slice(first * CELLS, (first + M_BACK) * CELLS)
        rows = [
            jnp.concatenate([ge_s[v, first * per + k : first * per + k + 1, :] for k in range(M_BACK * per)], axis=1)
            for v in range(2)
        ]
        dec_n = dec[:, cells]
        g, gs = gelu_pair(dot(w1[...], dec_n, TN) + bias1)
        dh = (w2_0 * rows[0] + w2_1 * rows[1]) * gs
        acc_b1 = acc_b1 + fold_lanes(dh)
        acc_w20 = acc_w20 + fold_lanes(g * rows[0])
        acc_w21 = acc_w21 + fold_lanes(g * rows[1])
        dh_a, dh_b = split2(dh)
        acc_w1 = acc_w1 + (dot(dec_n, dh_a, NT) + dot(dec_n, dh_b, NT))
        df = dot(w1[...], dh_a) + dot(w1[...], dh_b)
        cot = (df * slope[:, cells]).astype(BF16)
        cot_out[:, cells] = cot
        wide = cot.astype(F32)
        acc_cb = acc_cb + fold_lanes(wide)
        acc_cw = acc_cw + dot(ab_columns(wide), c_columns(side_by_side(bricks, first, M_BACK)), NT)
    lane = iota((ch, LANE), 1)
    tiles = [jnp.zeros((ch, LANE), F32) for _ in range(7)]
    pad = jnp.zeros((ch, LANE - 3 * ch), F32)
    for ab in range(9):
        block = jnp.concatenate([acc_cw[ab * ch : (ab + 1) * ch], pad], axis=1)
        tile, off = divmod(3 * ch * ab, LANE)
        if off == 0:
            tiles[tile] = tiles[tile] + block
        else:
            turned = pltpu.roll(block, off, 1)
            tiles[tile] = tiles[tile] + jnp.where(lane >= off, turned, 0.0)
            if tile + 1 < 7:
                tiles[tile + 1] = tiles[tile + 1] + jnp.where(lane < off, turned, 0.0)
    for k in range(7):
        payload_out[:, k, :] = tiles[k]
    small = [
        row_of(jnp.sum(acc_b1, axis=1, keepdims=True)),
        row_of(jnp.sum(acc_w20, axis=1, keepdims=True)),
        row_of(jnp.sum(acc_w21, axis=1, keepdims=True)),
        jnp.concatenate(
            [row_of(jnp.sum(acc_cb, axis=1, keepdims=True)), jnp.zeros((1, hid - ch), F32)], axis=1
        ),
        jnp.broadcast_to(loss[...], (1, hid)),
        jnp.zeros((ch - 5, hid), F32),
    ]
    payload_out[:, 7, :] = jnp.concatenate([acc_w1, jnp.concatenate(small, axis=0)], axis=1)


def bricks_back_kernel(cot, conv_w, out):
    count, ch = out.shape[0], out.shape[1]
    wf = offset_rows(conv_w)
    for first in range(0, count, M_GRAD):
        wide = cot[:, first * CELLS : (first + M_GRAD) * CELLS].astype(F32)
        z = dot(wf, ab_columns(wide), TN)
        total = z[ch : 2 * ch]
        total = total + shift_cells(z[0:ch], 1, 1) + shift_cells(z[2 * ch : 3 * ch], -1, 1)
        for n in range(M_GRAD):
            out[first + n] = total[:, n * CELLS : (n + 1) * CELLS].astype(BF16)


def add_kernel(values, out):
    total = values[0]
    for k in range(1, values.shape[0]):
        total = total + values[k]
    for k in range(out.shape[0]):
        out[k] = total


def finish_kernel(rays, values, cw_out, cb_out, w1_out, b1_out, w2_out, loss_out):
    ch = values.shape[0]
    hid = b1_out.shape[1]
    for k in range(7):
        width = min(LANE, cw_out.shape[1] - k * LANE)
        cw_out[:, k * LANE : k * LANE + width] = values[:, k, 0:width]
    small = values[:, 7, :]
    w1_out[...] = small[:, 0:hid]
    turned = pltpu.roll(small, LANE - hid, 1)
    b1_out[...] = turned[0:1, 0:hid]
    w2_out[...] = turned[1:3, 0:hid]
    cb_out[...] = turned[3:4, 0:ch]
    loss_out[...] = turned[4:5, 0:1] * (1.0 / rays)


VMEM = pl.BlockSpec(memory_space=pltpu.VMEM)
SMEM = pl.BlockSpec(memory_space=pltpu.SMEM)


def call(kernel, shapes, specs, args, scratch=(), name=None, flops=0, moved_bytes=0, out_specs=None):
    shapes = [jax.ShapeDtypeStruct(s, t) for s, t in shapes]
    return pl.pallas_call(
        kernel,
        out_shape=shapes,
        in_specs=specs,
        out_specs=out_specs or [VMEM] * len(shapes),
        scratch_shapes=list(scratch),
        name=name,
        cost_estimate=pl.CostEstimate(flops=flops, bytes_accessed=moved_bytes, transcendentals=0),
        compiler_params=pltpu.CompilerParams(vmem_limit_bytes=16 * 1024 * 1024),
    )(*args)


def swap(value, axis):
    return lax.all_to_all(value, axis, split_axis=0, concat_axis=0, tiled=True)


def local(
    bricks, conv_w, conv_b, head_w1, head_b1, head_w2, queries, sample_src, depth_target, inten_target, drop_label
):
    shells = lax.axis_size("shell")
    sectors = lax.axis_size("sector")
    shell = lax.axis_index("shell").astype(jnp.int32).reshape(1)
    blocks = bricks[0]
    count, ch = blocks.shape[0], blocks.shape[1]
    hid = head_w1.shape[1]
    cells = count * CELLS
    groups = cells // HI
    rays = depth_target.shape[0]
    b1 = head_b1.reshape(1, hid)
    w2t = head_w2.T
    operands = (blocks, conv_w, conv_b.reshape(1, ch), head_w1, b1, w2t)
    addr = swap(queries[0].reshape(sectors, 1, HI), "sector")
    dec, slope, planes, factor = call(
        decode_kernel,
        [((ch, cells), BF16), ((ch, cells), F32), ((6 * groups, HI), BF16), ((2, groups, HI), F32)],
        [VMEM] * 6,
        operands,
        scratch=[pltpu.VMEM((groups, HI), F32), pltpu.VMEM((groups, HI), F32)],
        name="decode",
        flops=2 * 10**9,
        moved_bytes=2 * 10**6,
    )
    (picked,) = call(
        owner_pick_kernel,
        [((sectors, 4, LANE), F32)],
        [VMEM] * 2,
        (addr, planes),
        name="owner_pick",
        flops=10**9,
        moved_bytes=10**5,
    )
    targets, slots = call(
        arrange_kernel,
        [((3, rays), F32), ((SAMP, rays), jnp.int32)],
        [VMEM] * 4,
        (
            depth_target.reshape(1, rays),
            inten_target.reshape(1, rays),
            drop_label.reshape(1, rays),
            lax.optimization_barrier((sample_src, picked))[0],
        ),
        name="arrange",
        flops=10**9,
        moved_bytes=10**5,
    )
    replies = swap(picked, "sector")
    density, intensity, terms = call(
        functools.partial(sample_kernel, shells),
        [((SAMP, rays), F32), ((SAMP, rays), F32), ((shells, 4, rays), F32)],
        [SMEM, VMEM, VMEM],
        (shell, replies, slots),
        name="sample",
        flops=10**9,
        moved_bytes=10**5,
    )
    terms = swap(terms, "shell")
    buckets, ray_depth, loss = call(
        functools.partial(render_kernel, shells),
        [((sectors, 4, LANE), F32), ((1, rays), F32), ((1, 1), F32)],
        [SMEM] + [VMEM] * 5,
        (shell, terms, density, intensity, slots, targets),
        name="render",
        flops=10**9,
        moved_bytes=10**5,
    )
    cots = swap(buckets, "sector")
    payload, conv_cot = call(
        owner_back_kernel,
        [((ch, 8, LANE), F32), ((ch, cells), BF16)],
        [VMEM] * 10,
        (addr, cots, factor, dec, slope, blocks, head_w1, b1, w2t, loss),
        scratch=[pltpu.VMEM((6, sectors, HI), F32), pltpu.VMEM((2, groups, HI), F32)],
        name="owner_back",
        flops=2 * 10**9,
        moved_bytes=2 * 10**6,
    )
    share = (ch * 8 // sectors, LANE)
    part = swap(payload.reshape((sectors,) + share), "sector")
    (brick_grads,) = call(
        bricks_back_kernel,
        [(blocks.shape, BF16)],
        [VMEM] * 2,
        (conv_cot, conv_w),
        name="bricks_back",
        flops=2 * 10**9,
        moved_bytes=10**6,
    )
    (part,) = call(add_kernel, [((shells,) + share, F32)], [VMEM], (part,), name="add_sectors")
    part = swap(part, "shell")
    (part,) = call(add_kernel, [((sectors,) + share, F32)], [VMEM], (part,), name="add_shells")
    whole = swap(part, "sector").reshape(ch, 8, LANE)
    conv_grad, conv_b_grad, grad_one, grad_b1, grad_two, loss_mean = call(
        functools.partial(finish_kernel, rays * sectors),
        [
            (conv_w.shape, F32),
            ((1, ch), F32),
            (head_w1.shape, F32),
            ((1, hid), F32),
            (w2t.shape, F32),
            ((1, 1), F32),
        ],
        [VMEM],
        (whole,),
        name="finish",
    )
    return (
        loss_mean.reshape(()),
        conv_grad,
        conv_b_grad.reshape(ch),
        grad_one,
        grad_b1.reshape(hid),
        grad_two.T,
        brick_grads[None],
        ray_depth.reshape(rays),
    )


def solution(mesh):
    return jax.shard_map(
        local,
        mesh=mesh,
        in_specs=(
            P("shell", "sector", None, None),
            P(),
            P(),
            P(),
            P(),
            P(),
            P("shell", "sector", None),
            P("shell", "sector"),
            P("sector"),
            P("sector"),
            P("sector"),
        ),
        out_specs=(P(), P(), P(), P(), P(), P(), P("shell", "sector", None, None), P("sector")),
        check_vma=False,
    )
```

```python
import functools

import jax
import jax.numpy as jnp
from jax import lax
from jax.experimental import pallas as pl
from jax.experimental.pallas import tpu as pltpu
from jax.sharding import PartitionSpec as P

SAMP = 8
CELLS = 512
LANE = 128
HI = 256
GELU_C = 0.7978845608028654
GELU_A = 0.044715

M_DECODE, M_BACK, M_GRAD, U_SPREAD = 8, 8, 4, 16

F32 = jnp.float32
BF16 = jnp.bfloat16
NT = (((1,), (1,)), ((), ()))
TN = (((0,), (0,)), ((), ()))
NN = (((1,), (0,)), ((), ()))


def dot(a, b, dims=NN):
    return lax.dot_general(a, b, dims, preferred_element_type=F32)


def iota(shape, axis):
    return lax.broadcasted_iota(jnp.int32, shape, axis)


def gelu_pair(x):
    x2 = x * x
    t = jnp.tanh(GELU_C * (x + GELU_A * (x2 * x)))
    half = 0.5 * (1.0 + t)
    slope = half + 0.5 * x * (1.0 - t * t) * (GELU_C * (1.0 + 3.0 * GELU_A * x2))
    return x * half, slope


def split3(v):
    a = v.astype(BF16).astype(F32)
    r = v - a
    b = r.astype(BF16).astype(F32)
    c = (r - b).astype(BF16).astype(F32)
    return a, b, c


def split2(v):
    a = v.astype(BF16)
    return a, (v - a.astype(F32)).astype(BF16)


def column(row):
    n = row.shape[1]
    eye = iota((n, n), 0) == iota((n, n), 1)
    return jnp.sum(jnp.where(eye, row, 0.0), axis=1, keepdims=True)


def row_of(col):
    n = col.shape[0]
    eye = iota((n, n), 0) == iota((n, n), 1)
    return jnp.sum(jnp.where(eye, col, 0.0), axis=0, keepdims=True)


def moved(x, step):
    return pltpu.roll(x, (-step) % x.shape[1], 1)


def shift_cells(x, direction, stride):
    if direction == 0:
        return x
    pos = (iota((1, x.shape[1]), 1) // stride) & 7
    ok = (pos >= 1) if direction < 0 else (pos <= 6)
    return jnp.where(ok, moved(x, direction * stride), 0.0)


def c_columns(block):
    wide = block.astype(F32)
    return jnp.concatenate([shift_cells(wide, c - 1, 1) for c in range(3)], axis=0).astype(BF16)


def ab_columns(cot):
    parts = []
    for a in range(3):
        part = shift_cells(cot, 1 - a, 64)
        for b in range(3):
            parts.append(shift_cells(part, 1 - b, 8))
    return jnp.concatenate(parts, axis=0).astype(BF16)


def offset_rows(conv_w):
    ch = conv_w.shape[0]
    width = 3 * ch
    wide = conv_w[...].astype(F32)
    tiles = [wide[:, k * LANE : (k + 1) * LANE] for k in range(wide.shape[1] // LANE)]
    lane = iota((ch, LANE), 1)
    rows = []
    for ab in range(9):
        tile, off = divmod(width * ab, LANE)
        if off == 0:
            rows.append(wide[:, tile * LANE : tile * LANE + width])
            continue
        block = pltpu.roll(tiles[tile], LANE - off, 1)
        if off + width > LANE:
            block = jnp.where(lane < LANE - off, block, pltpu.roll(tiles[tile + 1], LANE - off, 1))
        rows.append(block[:, 0:width])
    return jnp.concatenate(rows, axis=0).astype(BF16)


def side_by_side(bricks, first, number):
    return jnp.concatenate([bricks[first + n] for n in range(number)], axis=1)


def decode_kernel(bricks, conv_w, conv_b, w1, b1, w2t, dec_out, slope_out, planes_out, factor_out, e0_s, e1_s):
    count, ch = bricks.shape[0], bricks.shape[1]
    bias = column(conv_b[...])
    bias1 = column(b1[...])
    w2_0, w2_1 = column(w2t[0:1, :]), column(w2t[1:2, :])
    wf = offset_rows(conv_w)

    for first in range(0, count, M_DECODE):
        cells = slice(first * CELLS, (first + M_DECODE) * CELLS)
        y = dot(wf, c_columns(side_by_side(bricks, first, M_DECODE)))
        pre = bias
        for a in range(3):
            rows = [y[(3 * a + b) * ch : (3 * a + b + 1) * ch] for b in range(3)]
            t = rows[1] + shift_cells(rows[0], -1, 8) + shift_cells(rows[2], 1, 8)
            pre = pre + shift_cells(t, a - 1, 64)
        value, slope = gelu_pair(pre)
        dec = value.astype(BF16)
        dec_out[:, cells] = dec
        slope_out[:, cells] = slope
        g = gelu_pair(dot(w1[...], dec, TN) + bias1)[0]
        for w, e_s in ((w2_0, e0_s), (w2_1, e1_s)):
            e = jnp.sum(w * g, axis=0, keepdims=True)
            for k in range(M_DECODE * CELLS // HI):
                at = first * (CELLS // HI) + k
                e_s[at : at + 1, :] = e[:, k * HI : (k + 1) * HI]
    e0 = e0_s[...]
    e1 = e1_s[...]
    density = jnp.maximum(e0, 0.0) + jnp.log1p(jnp.exp(-jnp.abs(e0)))
    intensity = 1.0 / (1.0 + jnp.exp(-e1))
    factor_out[0] = 1.0 / (1.0 + jnp.exp(-e0))
    factor_out[1] = intensity * (1.0 - intensity)
    planes_out[...] = jnp.concatenate(split3(density) + split3(intensity), axis=0).astype(BF16)


def rays_last(sources):
    width = SAMP * LANE // 2
    rays = sources.shape[1] // SAMP
    lane = iota((SAMP, width), 1)
    mine = (lane & (SAMP - 1)) == iota((SAMP, width), 0)
    chosen = (iota((width, LANE // 2), 0) >> 3) == iota((width, LANE // 2), 1)
    chosen = jnp.where(chosen, 1.0, 0.0).astype(BF16)
    blocks = [jnp.where(mine, sources[:, k * width : (k + 1) * width], 0) for k in range(2 * rays // LANE)]
    stack = jnp.concatenate(blocks, axis=0)
    high = dot((stack >> 8).astype(F32).astype(BF16), chosen)
    low = dot((stack & 255).astype(F32).astype(BF16), chosen)
    whole = (high * 256.0 + low).astype(jnp.int32)
    parts = [whole[k * SAMP : (k + 1) * SAMP] for k in range(2 * rays // LANE)]
    return jnp.concatenate(parts, axis=1)


def arrange_kernel(target, inten_target, drop, sources, bricks, targets_out, slots_out, columns_out):
    columns_out[...] = c_columns(side_by_side(bricks, 0, bricks.shape[0]))
    targets_out[0:1, :] = target[...]
    targets_out[1:2, :] = inten_target[...]
    targets_out[2:3, :] = drop[...].astype(F32)
    slots_out[...] = rays_last(sources)


def one_hot(low):
    return jnp.where(iota((HI, low.shape[1]), 0) == low, 1.0, 0.0).astype(BF16)


def pick(planes, groups, address):
    found = dot(planes, one_hot(address & (HI - 1)))
    mine = iota((groups, address.shape[1]), 0) == (address >> 8)
    out = []
    for v in range(2):
        p = [found[(3 * v + k) * groups : (3 * v + k + 1) * groups] for k in range(3)]
        out.append(jnp.sum(jnp.where(mine, (p[0] + p[1]) + p[2], 0.0), axis=0, keepdims=True))
    return out


def spread(rows, groups, address):
    mine = iota((groups, address.shape[1]), 0) == (address >> 8)
    stack = jnp.concatenate([jnp.where(mine, r, 0.0) for r in rows], axis=0).astype(BF16)
    return dot(stack, one_hot(address & (HI - 1)), NT)


def join_planes(acc, groups):
    out = []
    for v in range(2):
        p = [acc[(3 * v + k) * groups : (3 * v + k + 1) * groups] for k in range(3)]
        out.append((p[0] + p[1]) + p[2])
    return out


def owner_pick_kernel(addr, planes, out):
    groups = planes.shape[0] // 6
    for s in range(addr.shape[0]):
        pair = pick(planes[...], groups, addr[s])
        for v in range(2):
            for half in range(2):
                out[s, 2 * v + half : 2 * v + half + 1, :] = pair[v][:, half * LANE : (half + 1) * LANE]


def excl_down(x):
    n = x.shape[0]
    at = iota(x.shape, 0)
    acc = jnp.where(at >= 1, pltpu.roll(x, 1, 0), 0.0)
    step = 1
    while step < n:
        acc = acc + jnp.where(at >= step, pltpu.roll(acc, step, 0), 0.0)
        step *= 2
    return acc


def excl_up(x):
    n = x.shape[0]
    at = iota(x.shape, 0)
    acc = jnp.where(at < n - 1, pltpu.roll(x, n - 1, 0), 0.0)
    step = 1
    while step < n:
        acc = acc + jnp.where(at < n - step, pltpu.roll(acc, n - step, 0), 0.0)
        step *= 2
    return acc


def sample_depths(shape, shell, shells):
    k = iota(shape, 0).astype(F32)
    return (shell.astype(F32) * SAMP + k + 0.5) / (shells * SAMP)


def sample_kernel(shells, shell_ref, replies, slots, density_out, intensity_out, out):
    groups = replies.shape[0]
    tables = [
        jnp.concatenate([replies[:, 2 * v, :], replies[:, 2 * v + 1, :]], axis=1) for v in range(2)
    ]
    planes = jnp.concatenate(split3(tables[0]) + split3(tables[1]), axis=0).astype(BF16)
    for k in range(SAMP):
        pair = pick(planes, groups, slots[k : k + 1, :])
        density_out[k : k + 1, :] = pair[0]
        intensity_out[k : k + 1, :] = pair[1]
    density = density_out[...]
    optical = density * (2.0 / (shells * SAMP))
    weights = jnp.exp(-excl_down(optical)) * (1.0 - jnp.exp(-optical))
    depth = jnp.sum(weights * sample_depths(density.shape, shell_ref[0], shells), axis=0, keepdims=True)
    inten = jnp.sum(weights * intensity_out[...], axis=0, keepdims=True)
    tau = jnp.sum(optical, axis=0, keepdims=True)
    packed = jnp.concatenate([depth, inten, tau, jnp.zeros_like(tau)], axis=0)
    for s in range(shells):
        out[s] = packed


def render_kernel(
    shells, shell_ref, terms, density, intensity, slots, targets, buckets_out, depth_out, loss_out
):
    shell = shell_ref[0]
    delta = 2.0 / (shells * SAMP)
    d_all = terms[:, 0, :]
    i_all = terms[:, 1, :]
    t_all = terms[:, 2, :]
    entry = jnp.exp(-excl_down(t_all))
    ray_depth = jnp.sum(entry * d_all, axis=0, keepdims=True)
    ray_inten = jnp.sum(entry * i_all, axis=0, keepdims=True)
    escape = jnp.exp(-jnp.sum(t_all, axis=0, keepdims=True))
    dropped = targets[2:3, :]
    kept = 1.0 - dropped
    depth_err = ray_depth - targets[0:1, :]
    inten_err = ray_inten - targets[1:2, :]
    loss = kept * (depth_err * depth_err + inten_err * inten_err) + (escape - dropped) * (escape - dropped)
    loss_out[...] = jnp.where(shell == 0, jnp.sum(loss, axis=1, keepdims=True), 0.0)
    depth_out[...] = ray_depth
    grad_depth = 2.0 * kept * depth_err
    grad_inten = 2.0 * kept * inten_err
    own = (grad_depth * d_all + grad_inten * i_all) * entry
    at = iota(own.shape, 0)
    behind = jnp.sum(jnp.where(at > shell, own, 0.0), axis=0, keepdims=True)
    entry_me = jnp.sum(jnp.where(at == shell, entry, 0.0), axis=0, keepdims=True)
    grad_tau = -2.0 * (escape - dropped) * escape - behind
    gd = grad_depth * entry_me
    gi = grad_inten * entry_me
    optical = density[...] * delta
    before = jnp.exp(-excl_down(optical))
    through = jnp.exp(-optical)
    weights = before * (1.0 - through)
    pull = gd * sample_depths(optical.shape, shell, shells) + gi * intensity[...]
    dens_grad = delta * (pull * before * through - excl_up(pull * weights) + grad_tau)
    inten_grad = gi * weights
    planes = split3(dens_grad) + split3(inten_grad)
    groups = buckets_out.shape[0]
    acc = jnp.zeros((6 * groups, HI), F32)
    for k in range(SAMP):
        acc = acc + spread([p[k : k + 1, :] for p in planes], groups, slots[k : k + 1, :])
    pair = join_planes(acc, groups)
    for v in range(2):
        for half in range(2):
            buckets_out[:, 2 * v + half, :] = pair[v][:, half * LANE : (half + 1) * LANE]


def fold_lanes(x):
    total = x[:, 0:LANE]
    for k in range(1, x.shape[1] // LANE):
        total = total + x[:, k * LANE : (k + 1) * LANE]
    return total


def owner_back_kernel(
    addr, cots, factor, dec, slope, columns, w1, b1, w2t, loss, payload_out, cot_out, plane_s, ge_s
):
    count, ch = dec.shape[1] // CELLS, dec.shape[0]
    hid = w1.shape[1]
    groups = factor.shape[1]
    sectors = addr.shape[0]
    for v in range(2):
        whole = jnp.concatenate([cots[:, 2 * v, :], cots[:, 2 * v + 1, :]], axis=1)
        for k, part in enumerate(split3(whole)):
            plane_s[3 * v + k] = part

    def body(s, acc):
        return acc + spread([plane_s[k, pl.ds(s, 1), :] for k in range(6)], groups, addr[s])

    acc = lax.fori_loop(0, sectors, body, jnp.zeros((6 * groups, HI), F32), unroll=U_SPREAD)
    pair = join_planes(acc, groups)
    for v in range(2):
        ge_s[v] = pair[v] * factor[v]
    bias1 = column(b1[...])
    w2_0, w2_1 = column(w2t[0:1, :]), column(w2t[1:2, :])
    per = CELLS // HI

    acc_w1 = jnp.zeros((ch, hid), F32)
    acc_b1 = jnp.zeros((hid, LANE), F32)
    acc_w20 = jnp.zeros((hid, LANE), F32)
    acc_w21 = jnp.zeros((hid, LANE), F32)
    acc_cb = jnp.zeros((ch, LANE), F32)
    acc_cw = jnp.zeros((9 * ch, 3 * ch), F32)
    for first in range(0, count, M_BACK):
        cells = slice(first * CELLS, (first + M_BACK) * CELLS)
        rows = [
            jnp.concatenate([ge_s[v, first * per + k : first * per + k + 1, :] for k in range(M_BACK * per)], axis=1)
            for v in range(2)
        ]
        dec_n = dec[:, cells]
        g, gs = gelu_pair(dot(w1[...], dec_n, TN) + bias1)
        dh = (w2_0 * rows[0] + w2_1 * rows[1]) * gs
        acc_b1 = acc_b1 + fold_lanes(dh)
        acc_w20 = acc_w20 + fold_lanes(g * rows[0])
        acc_w21 = acc_w21 + fold_lanes(g * rows[1])
        dh_a, dh_b = split2(dh)
        acc_w1 = acc_w1 + (dot(dec_n, dh_a, NT) + dot(dec_n, dh_b, NT))
        df = dot(w1[...], dh_a) + dot(w1[...], dh_b)
        cot = (df * slope[:, cells]).astype(BF16)
        cot_out[:, cells] = cot
        wide = cot.astype(F32)
        acc_cb = acc_cb + fold_lanes(wide)
        acc_cw = acc_cw + dot(ab_columns(wide), columns[:, cells], NT)
    lane = iota((ch, LANE), 1)
    tiles = [jnp.zeros((ch, LANE), F32) for _ in range(7)]
    pad = jnp.zeros((ch, LANE - 3 * ch), F32)
    for ab in range(9):
        block = jnp.concatenate([acc_cw[ab * ch : (ab + 1) * ch], pad], axis=1)
        tile, off = divmod(3 * ch * ab, LANE)
        if off == 0:
            tiles[tile] = tiles[tile] + block
        else:
            turned = pltpu.roll(block, off, 1)
            tiles[tile] = tiles[tile] + jnp.where(lane >= off, turned, 0.0)
            if tile + 1 < 7:
                tiles[tile + 1] = tiles[tile + 1] + jnp.where(lane < off, turned, 0.0)
    for k in range(7):
        payload_out[:, k, :] = tiles[k]
    small = [
        row_of(jnp.sum(acc_b1, axis=1, keepdims=True)),
        row_of(jnp.sum(acc_w20, axis=1, keepdims=True)),
        row_of(jnp.sum(acc_w21, axis=1, keepdims=True)),
        jnp.concatenate(
            [row_of(jnp.sum(acc_cb, axis=1, keepdims=True)), jnp.zeros((1, hid - ch), F32)], axis=1
        ),
        jnp.broadcast_to(loss[...], (1, hid)),
        jnp.zeros((ch - 5, hid), F32),
    ]
    payload_out[:, 7, :] = jnp.concatenate([acc_w1, jnp.concatenate(small, axis=0)], axis=1)


def bricks_back_kernel(cot, conv_w, out):
    count, ch = out.shape[0], out.shape[1]
    wf = offset_rows(conv_w)
    for first in range(0, count, M_GRAD):
        wide = cot[:, first * CELLS : (first + M_GRAD) * CELLS].astype(F32)
        z = dot(wf, ab_columns(wide), TN)
        total = z[ch : 2 * ch]
        total = total + shift_cells(z[0:ch], 1, 1) + shift_cells(z[2 * ch : 3 * ch], -1, 1)
        for n in range(M_GRAD):
            out[first + n] = total[:, n * CELLS : (n + 1) * CELLS].astype(BF16)


def add_kernel(values, out):
    total = values[0]
    for k in range(1, values.shape[0]):
        total = total + values[k]
    for k in range(out.shape[0]):
        out[k] = total


def finish_kernel(rays, values, cw_out, cb_out, w1_out, b1_out, w2_out, loss_out):
    ch = values.shape[0]
    hid = b1_out.shape[1]
    for k in range(7):
        width = min(LANE, cw_out.shape[1] - k * LANE)
        cw_out[:, k * LANE : k * LANE + width] = values[:, k, 0:width]
    small = values[:, 7, :]
    w1_out[...] = small[:, 0:hid]
    turned = pltpu.roll(small, LANE - hid, 1)
    b1_out[...] = turned[0:1, 0:hid]
    w2_out[...] = turned[1:3, 0:hid]
    cb_out[...] = turned[3:4, 0:ch]
    loss_out[...] = turned[4:5, 0:1] * (1.0 / rays)


VMEM = pl.BlockSpec(memory_space=pltpu.VMEM)
SMEM = pl.BlockSpec(memory_space=pltpu.SMEM)


def call(kernel, shapes, specs, args, scratch=(), name=None, flops=0, moved_bytes=0, out_specs=None):
    shapes = [jax.ShapeDtypeStruct(s, t) for s, t in shapes]
    return pl.pallas_call(
        kernel,
        out_shape=shapes,
        in_specs=specs,
        out_specs=out_specs or [VMEM] * len(shapes),
        scratch_shapes=list(scratch),
        name=name,
        cost_estimate=pl.CostEstimate(flops=flops, bytes_accessed=moved_bytes, transcendentals=0),
        compiler_params=pltpu.CompilerParams(vmem_limit_bytes=16 * 1024 * 1024),
    )(*args)


def swap(value, axis):
    return lax.all_to_all(value, axis, split_axis=0, concat_axis=0, tiled=True)


def local(
    bricks, conv_w, conv_b, head_w1, head_b1, head_w2, queries, sample_src, depth_target, inten_target, drop_label
):
    shells = lax.axis_size("shell")
    sectors = lax.axis_size("sector")
    shell = lax.axis_index("shell").astype(jnp.int32).reshape(1)
    blocks = bricks[0]
    count, ch = blocks.shape[0], blocks.shape[1]
    hid = head_w1.shape[1]
    cells = count * CELLS
    groups = cells // HI
    rays = depth_target.shape[0]
    b1 = head_b1.reshape(1, hid)
    w2t = head_w2.T
    operands = (blocks, conv_w, conv_b.reshape(1, ch), head_w1, b1, w2t)
    addr = swap(queries[0].reshape(sectors, 1, HI), "sector")
    dec, slope, planes, factor = call(
        decode_kernel,
        [((ch, cells), BF16), ((ch, cells), F32), ((6 * groups, HI), BF16), ((2, groups, HI), F32)],
        [VMEM] * 6,
        operands,
        scratch=[pltpu.VMEM((groups, HI), F32), pltpu.VMEM((groups, HI), F32)],
        name="decode",
        flops=2 * 10**9,
        moved_bytes=2 * 10**6,
    )
    (picked,) = call(
        owner_pick_kernel,
        [((sectors, 4, LANE), F32)],
        [VMEM] * 2,
        (addr, planes),
        name="owner_pick",
        flops=10**9,
        moved_bytes=10**5,
    )
    targets, slots, columns = call(
        arrange_kernel,
        [((3, rays), F32), ((SAMP, rays), jnp.int32), ((3 * ch, cells), BF16)],
        [VMEM] * 5,
        (
            depth_target.reshape(1, rays),
            inten_target.reshape(1, rays),
            drop_label.reshape(1, rays),
            lax.optimization_barrier((sample_src, picked))[0],
            blocks,
        ),
        name="arrange",
        flops=10**9,
        moved_bytes=10**5,
    )
    replies = swap(picked, "sector")
    density, intensity, terms = call(
        functools.partial(sample_kernel, shells),
        [((SAMP, rays), F32), ((SAMP, rays), F32), ((shells, 4, rays), F32)],
        [SMEM, VMEM, VMEM],
        (shell, replies, slots),
        name="sample",
        flops=10**9,
        moved_bytes=10**5,
    )
    terms = swap(terms, "shell")
    buckets, ray_depth, loss = call(
        functools.partial(render_kernel, shells),
        [((sectors, 4, LANE), F32), ((1, rays), F32), ((1, 1), F32)],
        [SMEM] + [VMEM] * 5,
        (shell, terms, density, intensity, slots, targets),
        name="render",
        flops=10**9,
        moved_bytes=10**5,
    )
    cots = swap(buckets, "sector")
    payload, conv_cot = call(
        owner_back_kernel,
        [((ch, 8, LANE), F32), ((ch, cells), BF16)],
        [VMEM] * 10,
        (addr, cots, factor, dec, slope, columns, head_w1, b1, w2t, loss),
        scratch=[pltpu.VMEM((6, sectors, HI), F32), pltpu.VMEM((2, groups, HI), F32)],
        name="owner_back",
        flops=2 * 10**9,
        moved_bytes=2 * 10**6,
    )
    share = (ch * 8 // sectors, LANE)
    part = swap(payload.reshape((sectors,) + share), "sector")
    (brick_grads,) = call(
        bricks_back_kernel,
        [(blocks.shape, BF16)],
        [VMEM] * 2,
        (conv_cot, conv_w),
        name="bricks_back",
        flops=2 * 10**9,
        moved_bytes=10**6,
    )
    (part,) = call(add_kernel, [((shells,) + share, F32)], [VMEM], (part,), name="add_sectors")
    part = swap(part, "shell")
    (part,) = call(add_kernel, [((sectors,) + share, F32)], [VMEM], (part,), name="add_shells")
    whole = swap(part, "sector").reshape(ch, 8, LANE)
    conv_grad, conv_b_grad, grad_one, grad_b1, grad_two, loss_mean = call(
        functools.partial(finish_kernel, rays * sectors),
        [
            (conv_w.shape, F32),
            ((1, ch), F32),
            (head_w1.shape, F32),
            ((1, hid), F32),
            (w2t.shape, F32),
            ((1, 1), F32),
        ],
        [VMEM],
        (whole,),
        name="finish",
    )
    return (
        loss_mean.reshape(()),
        conv_grad,
        conv_b_grad.reshape(ch),
        grad_one,
        grad_b1.reshape(hid),
        grad_two.T,
        brick_grads[None],
        ray_depth.reshape(rays),
    )


def solution(mesh):
    return jax.shard_map(
        local,
        mesh=mesh,
        in_specs=(
            P("shell", "sector", None, None),
            P(),
            P(),
            P(),
            P(),
            P(),
            P("shell", "sector", None),
            P("shell", "sector"),
            P("sector"),
            P("sector"),
            P("sector"),
        ),
        out_specs=(P(), P(), P(), P(), P(), P(), P("shell", "sector", None, None), P("sector")),
        check_vma=False,
    )
```
